32 devices in a mesh: groups: 2 (over y), expo: 4 (over z), tile: 4 (over x, core).
Axes of the slice: x: 2, y: 2, z: 4, core: 2. Of those that a mesh axis runs over, the one named last changes fastest.
Arguments:
- template: bfloat16 [8, 64, 4096], P(('groups', 'expo'), 'tile'), parts along dimension 0
- science: bfloat16 [8, 1, 64, 4096], P(('groups', 'expo'), None, 'tile'), parts along dimension 0
- plan: int32 [8], P('groups'), parts along dimension 0, may hold values from 0 to 3, as said below
- orders: int32 [6, 2], replicated, may hold values from 0 to 2
- coadd_weight: float32 [8, 1], P(('groups', 'expo')), parts along dimension 0, may hold values from 0.3 to 3
- intersection: int32 [8, 1], P(('groups', 'expo')), parts along dimension 0, may hold values 0 or 1
Outputs:
- coadd: float32 [2, 64, 4096], P('groups', 'tile', 'expo'), parts along dimension 0
- coeffs: float32 [8, 1, 13], P(('groups', 'expo')), parts along dimension 0
The draws below stay inside these ranges and needn't reach their ends.
There are 2 independent parts, one for each index of `groups`. The reference program is written for one: setup_inputs(seed, part) draws one part's arguments, and reference() takes and returns one part's arrays. A program takes and returns all parts, laid end to end along the dimension named above; an argument that names none is the same for every part. Nothing has to cross between parts.
Inputs may be any that keep to these rules, and one draw needn't show every extreme that they name: `plan`: a permutation of the group's patch indices.
All inputs are finite; a program needn't handle non-finite values. No bound on the sum of `intersection` on one device may be relied on, other than what follows from the above.
Results may differ from the reference program's by a relative error of at most 0.0061.
Values may be sent and summed in bfloat16 or wider, within the bound.
A program may use at most 64 MiB of HBM per device.

```python
import math
import jax
import jax.numpy as jnp
from jax import lax

W = 4096
HALF = 15
NB = 6
NU = 13
ROWS = 64
EXPOS = 4
PATCHES = 4
STEPS = 1


def template_field(key):
    field = jax.random.normal(jax.random.fold_in(key, 11), (PATCHES, ROWS, W), jnp.float32)
    return jnp.clip(field, -6.0, 6.0)


def plan_ids(key):
    order_ids = jax.random.permutation(jax.random.fold_in(key, 41), PATCHES)
    return order_ids.astype(jnp.int32)


def draw_template(key, part):
    return template_field(key).astype(jnp.bfloat16)


def draw_plan(key, part):
    return plan_ids(key)


def draw_science(key, part):
    field = template_field(key)
    picked = field[plan_ids(key)[:STEPS]]
    gains = jnp.exp(jax.random.uniform(jax.random.fold_in(key, 13), (EXPOS, STEPS), jnp.float32, -0.7, 0.7))
    shifts = jax.random.randint(jax.random.fold_in(key, 14), (EXPOS, STEPS, 2), -1, 2)
    noise = 0.5 * jax.random.normal(jax.random.fold_in(key, 15), (EXPOS, STEPS, ROWS, W), jnp.float32)

    def one_image(image, shift_pair):
        moved = jnp.roll(image, shift_pair[0], axis=0)
        return jnp.roll(moved, shift_pair[1], axis=1)
    moved_all = jax.vmap(jax.vmap(one_image, in_axes=(0, 0)), in_axes=(None, 0))(picked, shifts)
    return (gains[:, :, None, None] * moved_all + noise).astype(jnp.bfloat16)


def touch_ends(drawn, stream_key, least, high):
    longest = drawn.shape.index(max(drawn.shape))
    spots = []
    for shift in (0, 1):
        where = [jax.random.randint(jax.random.fold_in(stream_key, axis), (), 0, length) for axis, length in enumerate(drawn.shape)]
        where[longest] = (where[longest] + shift) % drawn.shape[longest]
        spots.append(tuple(where))
    return drawn.at[spots[0]].set(least).at[spots[1]].set(high)


def levels(stream_key, dims, split, smallest, largest):
    level, own = 1.0, jax.random.fold_in(stream_key, 6)
    for axis_at, blocks in split:
        draws = jnp.exp(jax.random.uniform(jax.random.fold_in(own, axis_at), (blocks,), jnp.float32, smallest / len(split), largest / len(split)))
        level = level * jnp.repeat(draws, dims[axis_at] // blocks).reshape([-1 if axis == axis_at else 1 for axis in range(len(dims))])
    return level


def setup_inputs(seed: int = 0, part: int = 0) -> dict:
    keys = jax.random.split(jax.random.key(seed), 7)
    part_keys = jax.random.split(jax.random.fold_in(keys[6], part), 7)
    return {
        "template": draw_template(jax.random.fold_in(jax.random.fold_in(keys[6], part), 71), part),
        "science": draw_science(jax.random.fold_in(jax.random.fold_in(keys[6], part), 71), part),
        "plan": draw_plan(jax.random.fold_in(jax.random.fold_in(keys[6], part), 71), part),
        "orders": touch_ends(jax.random.randint(keys[3], (NB, 2), 0, 3), jax.random.fold_in(keys[3], 1), 0, 2).astype(jnp.int32),
        "coadd_weight": jnp.clip(jnp.exp(math.log(3.0) - 2.3025851 * jax.random.uniform(part_keys[4], (EXPOS, STEPS), jnp.float32) ** levels(part_keys[4], (EXPOS, STEPS), ((0, 4),), -0.2, 0.2)), 0.3, 3.0),
        "intersection": touch_ends((jax.random.randint(part_keys[5], (EXPOS, STEPS), 0, 4) < 3).astype(jnp.int32), jax.random.fold_in(part_keys[5], 1), 0, 1),
    }


SIGMAS = (0.8, 1.4, 2.2, 3.0, 4.0, 5.5)
RIDGE = 0.05

def make_filters(orders):
    taps_pos = jnp.arange(2 * HALF + 1).astype(jnp.float32) - HALF
    row_list = []
    col_list = []
    for basis in range(NB):
        sigma = SIGMAS[basis]
        envelope = jnp.exp(-taps_pos * taps_pos / (2.0 * sigma * sigma))

        def power(order):
            return jnp.where(order == 0, 1.0, jnp.where(order == 1, taps_pos, taps_pos * taps_pos))
        row_filter = envelope * power(orders[basis, 0])
        col_filter = envelope * power(orders[basis, 1])
        row_list.append(row_filter / jnp.sqrt(jnp.sum(row_filter * row_filter)))
        col_list.append(col_filter / jnp.sqrt(jnp.sum(col_filter * col_filter)))
    return (jnp.stack(row_list).astype(jnp.bfloat16), jnp.stack(col_list).astype(jnp.bfloat16))

def convolve(patch, row_filters, col_filters):
    padded = jnp.pad(patch, ((HALF, HALF), (0, 0))).astype(jnp.float32)
    row_taps = row_filters.astype(jnp.float32)
    col_taps = col_filters.astype(jnp.float32)
    rowconv = jnp.zeros((NB, ROWS, W), jnp.float32)
    for tap in range(2 * HALF + 1):
        rowconv = rowconv + row_taps[:, tap][:, None, None] * padded[None, tap:tap + ROWS, :]
    rowconv = rowconv.astype(jnp.bfloat16)
    padded_cols = jnp.pad(rowconv, ((0, 0), (0, 0), (HALF, HALF))).astype(jnp.float32)
    conv = jnp.zeros((NB, ROWS, W), jnp.float32)
    for tap in range(2 * HALF + 1):
        conv = conv + col_taps[:, tap][:, None, None] * padded_cols[:, :, tap:tap + W]
    return conv

def reference(template, science, plan, orders, coadd_weight, intersection):
    row_filters, col_filters = make_filters(orders)
    column_pos = 2.0 * (jnp.arange(W).astype(jnp.float32) + 0.5) / W - 1.0
    coadds = []
    fitted = []
    for step in range(STEPS):
        patch = template[plan[step]]
        conv = convolve(patch, row_filters, col_filters)
        fields = jnp.concatenate([conv, conv * column_pos, jnp.ones((1, ROWS, W), jnp.float32)], axis=0)
        fields = fields.reshape(NU, ROWS * W)
        normal_matrix = jnp.dot(fields, fields.T, precision=lax.Precision.HIGHEST)
        normal_matrix = normal_matrix + RIDGE * (jnp.trace(normal_matrix) / NU) * jnp.eye(NU, dtype=jnp.float32)
        exposure_image = science[:, step].astype(jnp.float32).reshape(EXPOS, ROWS * W)
        projections = jnp.dot(exposure_image, fields.T, precision=lax.Precision.HIGHEST)
        factor = jnp.linalg.cholesky(normal_matrix)
        coeffs = jax.scipy.linalg.cho_solve((factor, True), projections.T).T
        model = jnp.dot(coeffs, fields, precision=lax.Precision.HIGHEST)
        difference = exposure_image - model
        weights = coadd_weight[:, step] * intersection[:, step].astype(jnp.float32)
        coadds.append(jnp.dot(weights, difference, precision=lax.Precision.HIGHEST).reshape(ROWS, W))
        fitted.append(coeffs)
    return (jnp.stack(coadds), jnp.stack(fitted, axis=1))
```

```python
import functools

import jax
import jax.numpy as jnp
from jax import lax
from jax.experimental import pallas as pl
from jax.experimental.pallas import tpu as pltpu
from jax.sharding import PartitionSpec as P

HALF = 15
NB = 6
NU = 13


SIGMAS = (0.8, 1.4, 2.2, 3.0, 4.0, 5.5)
RIDGE = 0.05


def broadcast(block, axis, holder):
    block = jnp.where(lax.axis_index(axis) == holder, block, jnp.zeros_like(block))
    return lax.psum(block, axis)


def extended(x, sides, width):
    for axis, dim in sides:
        size, length = (lax.axis_size(axis), x.shape[dim])
        up = [(i, (i + 1) % size) for i in range(size - 1)]
        down = [(j, i) for i, j in up]
        last = lax.slice_in_dim(x, length - width, length, axis=dim)
        first = lax.slice_in_dim(x, 0, width, axis=dim)
        before = lax.ppermute(last, axis, up)
        after = lax.ppermute(first, axis, down)
        x = jnp.concatenate([before, x, after], axis=dim)
    return x


def make_filters(orders):
    taps_pos = jnp.arange(2 * HALF + 1).astype(jnp.float32) - HALF
    row_list = []
    col_list = []
    for basis in range(NB):
        sigma = SIGMAS[basis]
        envelope = jnp.exp(-taps_pos * taps_pos / (2.0 * sigma * sigma))

        def power(order):
            return jnp.where(order == 0, 1.0, jnp.where(order == 1, taps_pos, taps_pos * taps_pos))

        row_filter = envelope * power(orders[basis, 0])
        col_filter = envelope * power(orders[basis, 1])
        row_list.append(row_filter / jnp.sqrt(jnp.sum(row_filter * row_filter)))
        col_list.append(col_filter / jnp.sqrt(jnp.sum(col_filter * col_filter)))
    return (jnp.stack(row_list).astype(jnp.bfloat16), jnp.stack(col_list).astype(jnp.bfloat16))


def band_matrix(filters, out_len, in_len):
    offset = jnp.arange(in_len)[None, :] - jnp.arange(out_len)[:, None]
    taps_idx = jnp.arange(2 * HALF + 1)
    picks = (offset[:, :, None] == taps_idx[None, None, :]).astype(jnp.float32)
    band = jnp.einsum("ijt,kt->kij", picks, filters.astype(jnp.float32))
    return band.astype(jnp.bfloat16)


def per_device(template, science, plan, orders, coadd_weight, intersection):
    row_filters, col_filters = make_filters(orders)
    rows = template.shape[1]
    width = template.shape[2]
    blocks_count = width // 128
    steps_count = science.shape[1]
    row_band = band_matrix(row_filters, rows, rows + 2 * HALF)
    col_band = jnp.transpose(band_matrix(col_filters, 128, 128 + 2 * HALF), (0, 2, 1))
    column_pos = 2.0 * (jnp.arange(width).astype(jnp.float32) + 0.5) / width - 1.0
    pieces = []
    fitted = []
    for step in range(steps_count):
        owner_index = plan[step]
        received = broadcast(template[0], "expo", owner_index)
        padded = extended(received, (("tile", 0),), HALF)
        rowconv = jnp.einsum(
            "kij,jw->kiw", row_band, padded, preferred_element_type=jnp.float32
        ).astype(jnp.bfloat16)
        blocks = rowconv.reshape(NB, rows, blocks_count, 128)
        empty_rim = jnp.zeros((NB, rows, 1, HALF), jnp.bfloat16)
        previous = jnp.concatenate([empty_rim, blocks[:, :, :-1, 128 - HALF :]], axis=2)
        following = jnp.concatenate([blocks[:, :, 1:, :HALF], empty_rim], axis=2)
        window = jnp.concatenate([previous, blocks, following], axis=3)
        conv = jnp.einsum("krbj,kjc->krbc", window, col_band, preferred_element_type=jnp.float32)
        conv = conv.reshape(NB, rows, width)
        fields = jnp.concatenate(
            [conv, conv * column_pos, jnp.ones((1, rows, width), jnp.float32)], axis=0
        )
        fields = fields.reshape(NU, rows * width)
        exposure_image = science[0, step].astype(jnp.float32).reshape(rows * width)
        normal_local = jnp.dot(fields, fields.T, precision=lax.Precision.HIGHEST)
        project_local = jnp.dot(fields, exposure_image, precision=lax.Precision.HIGHEST)
        normal_matrix, projections = lax.psum((normal_local, project_local), "tile")
        normal_matrix = normal_matrix + RIDGE * (jnp.trace(normal_matrix) / NU) * jnp.eye(
            NU, dtype=jnp.float32
        )
        factor = jnp.linalg.cholesky(normal_matrix)
        coeffs = jax.scipy.linalg.cho_solve((factor, True), projections)
        model = jnp.dot(coeffs, fields, precision=lax.Precision.HIGHEST)
        difference = exposure_image - model
        weight_now = coadd_weight[0, step] * intersection[0, step].astype(jnp.float32)
        pieces.append((weight_now * difference).reshape(rows, width))
        fitted.append(coeffs)
    weighted = jnp.stack(pieces)
    received_parts = lax.all_to_all(weighted[None], "expo", split_axis=3, concat_axis=0, tiled=True)
    coadd = jnp.sum(received_parts, axis=0)
    return (coadd, jnp.stack(fitted)[None])


LANES = 128
HALO = LANES // 2
VMEM_BYTES = 67043328
PAIRS = [(u, v) for u in range(NB) for v in range(u + 1)]
MESH = pl.DeviceIdType.MESH


def taps(position, sigma, order):
    power = jnp.where(order == 0, 1.0, jnp.where(order == 1, position, position * position))
    value = jnp.exp(-position * position / (2.0 * sigma * sigma)) * power
    return jnp.where(jnp.abs(position) <= HALF, value, 0.0)


def sublane_sums(tiles):
    row = lax.broadcasted_iota(jnp.int32, (8, LANES), 0)

    def merge(a, b, step):
        low = (row // step) % 2 == 0
        if step == 4:
            return jnp.where(low, a, b) + pltpu.roll(jnp.where(low, b, a), 4, 0)
        first = jnp.where(low, a, pltpu.roll(b, step, 0))
        return first + jnp.where(low, pltpu.roll(a, 8 - step, 0), b)

    fours = [merge(tiles[s], tiles[s + 4], 4) for s in range(4)]
    twos = [merge(fours[s], fours[s + 2], 2) for s in range(2)]
    return merge(twos[0], twos[1], 1)


def fused(
    dims,
    template_ref,
    science_ref,
    plan_ref,
    orders_ref,
    weight_ref,
    inter_ref,
    coadd_ref,
    coeffs_ref,
    tbuf,
    picked,
    sbuf,
    wbuf,
    rbuf,
    row_band,
    col_band,
    conv_ref,
    fold_ref,
    stat_ref,
    plan_mem,
    orders_mem,
    weight_mem,
    inter_mem,
    local_sem,
    tsend,
    trecv,
    ssend,
    srecv,
    wsend,
    wrecv,
    fsend,
    frecv,
    rsend,
    rrecv,
):
    expos, tiles, rows, width, cols = dims
    per = cols // LANES
    span = cols + 2 * LANES
    keep = cols + 2 * HALO
    me = lax.axis_index("expo")
    tile = lax.axis_index("tile")

    def others():
        near = [0] + list(range(2, expos - 1))
        for de in [expos - 1, 1][: expos - 1] + near[1:] + near[:1]:
            for dt in reversed(range(tiles)):
                if de or dt:
                    yield de * tiles + dt, (me + de) % expos, (tile + dt) % tiles

    barrier = pltpu.get_barrier_semaphore()

    for d in range(1, expos):
        peer = (me + d) % expos
        pl.semaphore_signal(barrier, inc=1, device_id={"expo": peer}, device_id_type=MESH)
    for d in (1, tiles - 1):
        peer = (tile + d) % tiles
        pl.semaphore_signal(barrier, inc=1, device_id={"tile": peer}, device_id_type=MESH)

    def source_start(e):
        return e * per - 1 + (expos - 1 - e) // (expos - 1) - e // (expos - 1)

    def source_columns(e):
        return pl.ds(pl.multiple_of(source_start(e) * LANES, LANES), span)

    def window_columns(e):
        return pl.ds(pl.multiple_of((source_start(e) - e * per + 2) * LANES, LANES), span)

    def own_columns(e):
        return pl.ds(pl.multiple_of(e * cols, LANES), cols)

    local = [
        pltpu.make_async_copy(plan_ref, plan_mem, local_sem.at[0]),
        pltpu.make_async_copy(orders_ref, orders_mem, local_sem.at[1]),
        pltpu.make_async_copy(weight_ref, weight_mem, local_sem.at[2]),
        pltpu.make_async_copy(inter_ref, inter_mem, local_sem.at[3]),
        pltpu.make_async_copy(
            template_ref.at[0, :, source_columns(me)],
            tbuf.at[me, :, window_columns(me)],
            local_sem.at[4],
        ),
        pltpu.make_async_copy(
            science_ref.at[0, 0, :, own_columns(me)], sbuf.at[me], local_sem.at[5]
        ),
    ]
    plan_in, orders_in, weight_in, inter_in, mine, mine_science = local
    for copy in local:
        copy.start()

    def template_copy(d, target, holder):
        return pltpu.make_async_remote_copy(
            src_ref=template_ref.at[0, :, source_columns(target)],
            dst_ref=tbuf.at[holder, :, window_columns(target)],
            send_sem=tsend.at[d],
            recv_sem=trecv.at[d],
            device_id={"expo": target},
            device_id_type=MESH,
        )

    def science_copy(d, target, holder):
        return pltpu.make_async_remote_copy(
            src_ref=science_ref.at[0, 0, :, own_columns(target)],
            dst_ref=sbuf.at[holder],
            send_sem=ssend.at[d],
            recv_sem=srecv.at[d],
            device_id={"expo": target},
            device_id_type=MESH,
        )

    def weight_copy(d, target, holder):
        return pltpu.make_async_remote_copy(
            src_ref=wbuf.at[holder],
            dst_ref=wbuf.at[holder],
            send_sem=wsend.at[d],
            recv_sem=wrecv.at[d],
            device_id={"expo": target},
            device_id_type=MESH,
        )

    def forward_copy(side):
        target = tile + 1 if side == 0 else tile - 1
        return pltpu.make_async_remote_copy(
            src_ref=picked.at[1],
            dst_ref=picked.at[2 * side],
            send_sem=fsend.at[side],
            recv_sem=frecv.at[side],
            device_id={"tile": target},
            device_id_type=MESH,
        )

    def stat_copy(index, e, t, to_e, to_t):
        return pltpu.make_async_remote_copy(
            src_ref=rbuf.at[e, t],
            dst_ref=rbuf.at[e, t],
            send_sem=rsend.at[index],
            recv_sem=rrecv.at[index],
            device_id={"expo": to_e, "tile": to_t},
            device_id_type=MESH,
        )

    pl.semaphore_wait(barrier, expos + 1)
    for d in reversed(range(1, expos)):
        template_copy(d, (me + d) % expos, me).start()

    for d in range(1, expos):
        science_copy(d, (me + d) % expos, me).start()
    weight_in.wait()
    inter_in.wait()
    weight = weight_mem[0, 0] * inter_mem[0, 0].astype(jnp.float32)
    wbuf[me] = jnp.full((1, LANES), weight, jnp.float32)
    for d in range(1, expos):
        weight_copy(d, (me + d) % expos, me).start()

    orders_in.wait()
    position = lax.broadcasted_iota(jnp.int32, (1, LANES), 1).astype(jnp.float32) - HALF
    for k in range(NB):
        sigma = SIGMAS[k]
        for side in range(2):
            order = orders_mem[side, k]
            line = taps(position, sigma, jnp.full((1, LANES), order, jnp.int32))
            scale = 1.0 / jnp.sqrt(jnp.sum(line * line, axis=1, keepdims=True))
            shape = (rows, 3 * rows) if side == 0 else (LANES + 2 * HALO, LANES)
            ahead = lax.broadcasted_iota(jnp.int32, shape, 1 - side)
            behind = lax.broadcasted_iota(jnp.int32, shape, side)
            offset = (ahead - behind - (rows if side == 0 else HALO)).astype(jnp.float32)
            band = taps(offset, sigma, jnp.full(shape, order, jnp.int32))
            band = (band * scale).astype(jnp.bfloat16)
            if side == 0:
                row_band[k * rows : (k + 1) * rows, :] = band
            else:
                col_band[k] = band

    @pl.when(tile == 0)
    def _():
        picked[0] = jnp.zeros((rows, keep), jnp.bfloat16)

    @pl.when(tile == tiles - 1)
    def _():
        picked[2] = jnp.zeros((rows, keep), jnp.bfloat16)

    plan_in.wait()
    owner = plan_mem[0]
    mine.wait()
    for d in range(1, expos):
        template_copy(d, me, (me + expos - d) % expos).wait_recv()

    block = tbuf[owner, :, LANES : LANES + span].astype(jnp.float32)
    place = jnp.full((rows, LANES), me, jnp.int32)
    block = jnp.concatenate(
        [
            jnp.where(place > 0, block[:, :LANES], 0.0),
            block[:, LANES : span - LANES],
            jnp.where(place < expos - 1, block[:, span - LANES :], 0.0),
        ],
        axis=1,
    )
    picked[1] = block[:, LANES - HALO : LANES - HALO + keep].astype(jnp.bfloat16)

    @pl.when(tile < tiles - 1)
    def _():
        forward_copy(0).start()

    @pl.when(tile > 0)
    def _():
        forward_copy(1).start()

    @pl.when(tile > 0)
    def _():
        forward_copy(0).wait_recv()

    @pl.when(tile < tiles - 1)
    def _():
        forward_copy(1).wait_recv()

    rowconv = jnp.dot(
        row_band[...], picked[...].reshape(3 * rows, keep), preferred_element_type=jnp.float32
    ).astype(jnp.bfloat16)
    for k in range(NB):
        mine_rows = rowconv[k * rows : (k + 1) * rows]
        windows = jnp.concatenate(
            [mine_rows[:, b * LANES : (b + 1) * LANES + 2 * HALO] for b in range(per)], axis=0
        )
        conv_ref[k] = jnp.dot(windows, col_band[k], preferred_element_type=jnp.float32)

    def conv_at(k, b):
        return conv_ref[k, b * rows : (b + 1) * rows, :]

    def science_at(e, b):
        return sbuf[e, :, b * LANES : (b + 1) * LANES].astype(jnp.float32)

    def fold(x):
        return x.reshape(rows // 8, 8, LANES).sum(axis=0)

    lane = lax.broadcasted_iota(jnp.int32, (1, LANES), 1)
    first = 2.0 * ((me * cols + lane).astype(jnp.float32) + 0.5) / width - 1.0
    pitch = 2.0 * LANES / width
    column = [first + b * pitch for b in range(per)]

    def running(tiles_of, depth):
        sums = [None] * depth
        for b in reversed(range(per)):
            carry = tiles_of(b)
            for level in range(depth):
                if level and b == 0:
                    break
                sums[level] = carry if sums[level] is None else sums[level] + carry
                carry = sums[level]
        return sums

    def once(sums):
        return first * sums[0] + pitch * sums[1]

    count = 3 * len(PAIRS) + 2 * NB
    first_twice = first * first
    first_once = 2.0 * pitch * first - pitch * pitch
    for index, (u, v) in enumerate(PAIRS):
        sums = running(lambda b: fold(conv_at(u, b) * conv_at(v, b)), 3)
        fold_ref[3 * index] = sums[0]
        fold_ref[3 * index + 1] = once(sums)
        fold_ref[3 * index + 2] = (
            first_twice * sums[0] + first_once * sums[1] + (2.0 * pitch * pitch) * sums[2]
        )
    for u in range(NB):
        sums = running(lambda b: fold(conv_at(u, b)), 2)
        fold_ref[3 * len(PAIRS) + u] = sums[0]
        fold_ref[3 * len(PAIRS) + NB + u] = once(sums)

    mine_science.wait()
    for d in range(1, expos):
        science_copy(d, me, (me + expos - d) % expos).wait_recv()
    for e in range(expos):
        science = [science_at(e, b) for b in range(per)]
        for u in range(NB):
            sums = running(lambda b: fold(conv_at(u, b) * science[b]), 2)
            fold_ref[count + u * expos + e] = sums[0]
            fold_ref[count + (NB + u) * expos + e] = once(sums)
        fold_ref[count + 2 * NB * expos + e] = running(lambda b: fold(science[b]), 1)[0]
    used = count + NU * expos
    for index in range(used, LANES):
        fold_ref[index] = jnp.zeros((8, LANES), jnp.float32)

    packed = jnp.concatenate(
        [sublane_sums([fold_ref[g + s] for s in range(8)]) for g in range(0, LANES, 8)], axis=0
    )
    rbuf[me, tile] = jnp.sum(jnp.transpose(packed), axis=0, keepdims=True)
    for index, e, t in others():
        stat_copy(index, me, tile, e, t).start()

    for d in range(1, expos):
        weight_copy(d, me, (me + expos - d) % expos).wait_recv()
    weights = [wbuf[e] for e in range(expos)]
    for b in range(per):
        result = science_at(0, b) * weights[0]
        for e in range(1, expos):
            result = result + science_at(e, b) * weights[e]
        coadd_ref[0, :, b * LANES : (b + 1) * LANES] = result

    for index, e, t in others():
        de, dt = index // tiles, index % tiles
        e = (me + expos - de) % expos
        t = (tile + tiles - dt) % tiles
        stat_copy(index, e, t, e, t).wait_recv()

    total = rbuf[0, 0]
    for e in range(expos):
        for t in range(tiles):
            if e or t:
                total = total + rbuf[e, t]
    stat_ref[...] = jnp.transpose(jnp.broadcast_to(total, (LANES, LANES)))

    def value(index):
        return jnp.broadcast_to(stat_ref[index : index + 1, :], (expos, LANES))

    matrix = [[None] * NU for _ in range(NU)]
    for index, (u, v) in enumerate(PAIRS):
        plain, linear, square = (value(3 * index + moment) for moment in range(3))
        matrix[u][v] = plain
        matrix[NB + u][v] = linear
        matrix[NB + v][u] = linear
        matrix[NB + u][NB + v] = square
    for u in range(2 * NB):
        matrix[2 * NB][u] = value(3 * len(PAIRS) + u)
    pixels = float(rows * tiles * width)
    matrix[2 * NB][2 * NB] = jnp.full((expos, LANES), pixels, jnp.float32)
    trace = matrix[0][0]
    for u in range(1, NU):
        trace = trace + matrix[u][u]
    ridge = RIDGE * (trace / NU)
    for u in range(NU):
        matrix[u][u] = matrix[u][u] + ridge
    right = [stat_ref[count + u * expos : count + (u + 1) * expos, :] for u in range(NU)]
    inverse = [None] * NU
    for j in range(NU):
        inverse[j] = 1.0 / matrix[j][j]
        for i in range(j + 1, NU):
            ratio = matrix[i][j] * inverse[j]
            for m in range(j + 1, i + 1):
                matrix[i][m] = matrix[i][m] - ratio * matrix[m][j]
            right[i] = right[i] - ratio * right[j]
    fitted = [None] * NU
    for j in reversed(range(NU)):
        left = right[j]
        for i in range(j + 1, NU):
            left = left - matrix[i][j] * fitted[i]
        fitted[j] = left * inverse[j]

    stacked = jnp.concatenate(weights, axis=0)
    joint = [jnp.sum(stacked * fitted[u], axis=0, keepdims=True) for u in range(NU)]
    for b in range(per):
        block = slice(b * LANES, (b + 1) * LANES)
        result = coadd_ref[0, :, block] - joint[2 * NB]
        for k in range(NB):
            factor = joint[k] + column[b] * joint[NB + k]
            result = result - conv_at(k, b) * factor
        coadd_ref[0, :, block] = result

    spread = lax.broadcasted_iota(jnp.int32, (expos, LANES), 1)
    table = jnp.zeros((expos, LANES), jnp.float32)
    for u in range(NU):
        table = jnp.where(spread == u, fitted[u], table)
    exposure = lax.broadcasted_iota(jnp.int32, (expos, LANES), 0)
    line = jnp.sum(jnp.where(exposure == me, table, 0.0), axis=0, keepdims=True)
    coeffs_ref[0] = line[:, :NU]

    for d in range(1, expos):
        template_copy(d, (me + d) % expos, me).wait_send()
        science_copy(d, (me + d) % expos, me).wait_send()
        weight_copy(d, (me + d) % expos, me).wait_send()

    @pl.when(tile < tiles - 1)
    def _():
        forward_copy(0).wait_send()

    @pl.when(tile > 0)
    def _():
        forward_copy(1).wait_send()

    for index, e, t in others():
        stat_copy(index, me, tile, e, t).wait_send()


def store(coadd_in, coeffs_in, coadd_out, coeffs_out, sem):
    copies = [
        pltpu.make_async_copy(coadd_in, coadd_out, sem.at[0]),
        pltpu.make_async_copy(coeffs_in, coeffs_out, sem.at[1]),
    ]
    for copy in copies:
        copy.start()
    for copy in copies:
        copy.wait()


def window(sizes, template, science, plan, orders, coadd_weight, intersection):
    expos, tiles = (sizes["expo"], sizes["tile"])
    rows, width = template.shape[1:]
    cols = width // expos
    fits = (
        science.shape[1] == 1
        and template.shape[0] == 1
        and expos > 2
        and tiles > 2
        and width % expos == 0
        and cols % LANES == 0
        and cols // LANES > 2
        and rows % 16 == 0
        and 3 * len(PAIRS) + 2 * NB + NU * expos <= LANES
    )
    if not fits:
        return per_device(template, science, plan, orders, coadd_weight, intersection)
    spare = 10368 * 1024
    dims = (expos, tiles, rows, width, cols)
    dma = pltpu.SemaphoreType.DMA
    far = pl.BlockSpec(memory_space=pltpu.HBM)
    vector = pl.BlockSpec(memory_space=pltpu.VMEM)
    shapes = (
        jax.ShapeDtypeStruct((1, rows, cols), jnp.float32),
        jax.ShapeDtypeStruct((1, 1, NU), jnp.float32),
    )
    orders = orders.T
    results = pl.pallas_call(
        functools.partial(fused, dims),
        out_shape=shapes,
        in_specs=[far] * 6,
        out_specs=(vector, vector),
        scratch_shapes=[
            pltpu.VMEM((expos, rows, cols + 4 * LANES), jnp.bfloat16),
            pltpu.VMEM((3, rows, cols + 2 * HALO), jnp.bfloat16),
            pltpu.VMEM((expos, rows, cols), jnp.bfloat16),
            pltpu.VMEM((expos, 1, LANES), jnp.float32),
            pltpu.VMEM((expos, tiles, 1, LANES), jnp.float32),
            pltpu.VMEM((NB * rows, 3 * rows), jnp.bfloat16),
            pltpu.VMEM((NB, LANES + 2 * HALO, LANES), jnp.bfloat16),
            pltpu.VMEM((NB, rows * (cols // LANES), LANES), jnp.float32),
            pltpu.VMEM((LANES, 8, LANES), jnp.float32),
            pltpu.VMEM((LANES, LANES), jnp.float32),
            pltpu.SMEM(plan.shape, jnp.int32),
            pltpu.SMEM(orders.shape, jnp.int32),
            pltpu.SMEM(coadd_weight.shape, jnp.float32),
            pltpu.SMEM(intersection.shape, jnp.int32),
            dma((6,)),
            dma((expos,)),
            dma((expos,)),
            dma((expos,)),
            dma((expos,)),
            dma((expos,)),
            dma((expos,)),
            dma((2,)),
            dma((2,)),
            dma((expos * tiles,)),
            dma((expos * tiles,)),
        ],
        compiler_params=pltpu.CompilerParams(
            collective_id=0, has_side_effects=True, vmem_limit_bytes=VMEM_BYTES - spare
        ),
    )(template, science, plan, orders, coadd_weight, intersection)
    return pl.pallas_call(
        store,
        out_shape=shapes,
        in_specs=[vector, vector],
        out_specs=(far, far),
        scratch_shapes=[dma((2,))],
        compiler_params=pltpu.CompilerParams(vmem_limit_bytes=1024 * 1024),
    )(*results)


def solution(mesh):
    return jax.shard_map(
        functools.partial(window, dict(mesh.shape)),
        mesh=mesh,
        in_specs=(
            P(("groups", "expo"), "tile", None),
            P(("groups", "expo"), None, "tile", None),
            P("groups"),
            P(),
            P(("groups", "expo"), None),
            P(("groups", "expo"), None),
        ),
        out_specs=(P("groups", "tile", "expo"), P(("groups", "expo"), None, None)),
        check_vma=False,
    )
```

```python
import functools

import jax
import jax.numpy as jnp
from jax import lax
from jax.experimental import pallas as pl
from jax.experimental.pallas import tpu as pltpu
from jax.sharding import PartitionSpec as P

HALF = 15
NB = 6
NU = 13


SIGMAS = (0.8, 1.4, 2.2, 3.0, 4.0, 5.5)
RIDGE = 0.05


def broadcast(block, axis, holder):
    block = jnp.where(lax.axis_index(axis) == holder, block, jnp.zeros_like(block))
    return lax.psum(block, axis)


def extended(x, sides, width):
    for axis, dim in sides:
        size, length = (lax.axis_size(axis), x.shape[dim])
        up = [(i, (i + 1) % size) for i in range(size - 1)]
        down = [(j, i) for i, j in up]
        last = lax.slice_in_dim(x, length - width, length, axis=dim)
        first = lax.slice_in_dim(x, 0, width, axis=dim)
        before = lax.ppermute(last, axis, up)
        after = lax.ppermute(first, axis, down)
        x = jnp.concatenate([before, x, after], axis=dim)
    return x


def make_filters(orders):
    taps_pos = jnp.arange(2 * HALF + 1).astype(jnp.float32) - HALF
    row_list = []
    col_list = []
    for basis in range(NB):
        sigma = SIGMAS[basis]
        envelope = jnp.exp(-taps_pos * taps_pos / (2.0 * sigma * sigma))

        def power(order):
            return jnp.where(order == 0, 1.0, jnp.where(order == 1, taps_pos, taps_pos * taps_pos))

        row_filter = envelope * power(orders[basis, 0])
        col_filter = envelope * power(orders[basis, 1])
        row_list.append(row_filter / jnp.sqrt(jnp.sum(row_filter * row_filter)))
        col_list.append(col_filter / jnp.sqrt(jnp.sum(col_filter * col_filter)))
    return (jnp.stack(row_list).astype(jnp.bfloat16), jnp.stack(col_list).astype(jnp.bfloat16))


def band_matrix(filters, out_len, in_len):
    offset = jnp.arange(in_len)[None, :] - jnp.arange(out_len)[:, None]
    taps_idx = jnp.arange(2 * HALF + 1)
    picks = (offset[:, :, None] == taps_idx[None, None, :]).astype(jnp.float32)
    band = jnp.einsum("ijt,kt->kij", picks, filters.astype(jnp.float32))
    return band.astype(jnp.bfloat16)


def per_device(template, science, plan, orders, coadd_weight, intersection):
    row_filters, col_filters = make_filters(orders)
    rows = template.shape[1]
    width = template.shape[2]
    blocks_count = width // 128
    steps_count = science.shape[1]
    row_band = band_matrix(row_filters, rows, rows + 2 * HALF)
    col_band = jnp.transpose(band_matrix(col_filters, 128, 128 + 2 * HALF), (0, 2, 1))
    column_pos = 2.0 * (jnp.arange(width).astype(jnp.float32) + 0.5) / width - 1.0
    pieces = []
    fitted = []
    for step in range(steps_count):
        owner_index = plan[step]
        received = broadcast(template[0], "expo", owner_index)
        padded = extended(received, (("tile", 0),), HALF)
        rowconv = jnp.einsum(
            "kij,jw->kiw", row_band, padded, preferred_element_type=jnp.float32
        ).astype(jnp.bfloat16)
        blocks = rowconv.reshape(NB, rows, blocks_count, 128)
        empty_rim = jnp.zeros((NB, rows, 1, HALF), jnp.bfloat16)
        previous = jnp.concatenate([empty_rim, blocks[:, :, :-1, 128 - HALF :]], axis=2)
        following = jnp.concatenate([blocks[:, :, 1:, :HALF], empty_rim], axis=2)
        window = jnp.concatenate([previous, blocks, following], axis=3)
        conv = jnp.einsum("krbj,kjc->krbc", window, col_band, preferred_element_type=jnp.float32)
        conv = conv.reshape(NB, rows, width)
        fields = jnp.concatenate(
            [conv, conv * column_pos, jnp.ones((1, rows, width), jnp.float32)], axis=0
        )
        fields = fields.reshape(NU, rows * width)
        exposure_image = science[0, step].astype(jnp.float32).reshape(rows * width)
        normal_local = jnp.dot(fields, fields.T, precision=lax.Precision.HIGHEST)
        project_local = jnp.dot(fields, exposure_image, precision=lax.Precision.HIGHEST)
        normal_matrix, projections = lax.psum((normal_local, project_local), "tile")
        normal_matrix = normal_matrix + RIDGE * (jnp.trace(normal_matrix) / NU) * jnp.eye(
            NU, dtype=jnp.float32
        )
        factor = jnp.linalg.cholesky(normal_matrix)
        coeffs = jax.scipy.linalg.cho_solve((factor, True), projections)
        model = jnp.dot(coeffs, fields, precision=lax.Precision.HIGHEST)
        difference = exposure_image - model
        weight_now = coadd_weight[0, step] * intersection[0, step].astype(jnp.float32)
        pieces.append((weight_now * difference).reshape(rows, width))
        fitted.append(coeffs)
    weighted = jnp.stack(pieces)
    received_parts = lax.all_to_all(weighted[None], "expo", split_axis=3, concat_axis=0, tiled=True)
    coadd = jnp.sum(received_parts, axis=0)
    return (coadd, jnp.stack(fitted)[None])


LANES = 128
HALO = LANES // 2
VMEM_BYTES = 67043328
PAIRS = [(u, v) for u in range(NB) for v in range(u + 1)]
MESH = pl.DeviceIdType.MESH


def taps(position, sigma, order):
    power = jnp.where(order == 0, 1.0, jnp.where(order == 1, position, position * position))
    value = jnp.exp(-position * position / (2.0 * sigma * sigma)) * power
    return jnp.where(jnp.abs(position) <= HALF, value, 0.0)


def sublane_sums(tiles):
    row = lax.broadcasted_iota(jnp.int32, (8, LANES), 0)

    def merge(a, b, step):
        low = (row // step) % 2 == 0
        if step == 4:
            return jnp.where(low, a, b) + pltpu.roll(jnp.where(low, b, a), 4, 0)
        first = jnp.where(low, a, pltpu.roll(b, step, 0))
        return first + jnp.where(low, pltpu.roll(a, 8 - step, 0), b)

    fours = [merge(tiles[s], tiles[s + 4], 4) for s in range(4)]
    twos = [merge(fours[s], fours[s + 2], 2) for s in range(2)]
    return merge(twos[0], twos[1], 1)


def fused(
    dims,
    template_ref,
    science_ref,
    plan_ref,
    orders_ref,
    weight_ref,
    inter_ref,
    coadd_ref,
    coeffs_ref,
    tbuf,
    picked,
    sbuf,
    wbuf,
    rbuf,
    row_band,
    col_band,
    conv_ref,
    fold_ref,
    stat_ref,
    plan_mem,
    orders_mem,
    weight_mem,
    inter_mem,
    local_sem,
    tsend,
    trecv,
    ssend,
    srecv,
    wsend,
    wrecv,
    fsend,
    frecv,
    rsend,
    rrecv,
):
    expos, tiles, rows, width, cols = dims
    per = cols // LANES
    span = cols + 2 * LANES
    keep = cols + 2 * HALO
    me = lax.axis_index("expo")
    tile = lax.axis_index("tile")

    def others():
        near = [0] + list(range(2, expos - 1))
        for de in [expos - 1, 1][: expos - 1] + near[1:] + near[:1]:
            for dt in reversed(range(tiles)):
                if de or dt:
                    yield de * tiles + dt, (me + de) % expos, (tile + dt) % tiles

    barrier = pltpu.get_barrier_semaphore()

    for d in range(1, expos):
        peer = (me + d) % expos
        pl.semaphore_signal(barrier, inc=1, device_id={"expo": peer}, device_id_type=MESH)
    for d in (1, tiles - 1):
        peer = (tile + d) % tiles
        pl.semaphore_signal(barrier, inc=1, device_id={"tile": peer}, device_id_type=MESH)

    def source_start(e):
        return e * per - 1 + (expos - 1 - e) // (expos - 1) - e // (expos - 1)

    def source_columns(e):
        return pl.ds(pl.multiple_of(source_start(e) * LANES, LANES), span)

    def window_columns(e):
        return pl.ds(pl.multiple_of((source_start(e) - e * per + 2) * LANES, LANES), span)

    def own_columns(e):
        return pl.ds(pl.multiple_of(e * cols, LANES), cols)

    local = [
        pltpu.make_async_copy(plan_ref, plan_mem, local_sem.at[0]),
        pltpu.make_async_copy(orders_ref, orders_mem, local_sem.at[1]),
        pltpu.make_async_copy(weight_ref, weight_mem, local_sem.at[2]),
        pltpu.make_async_copy(inter_ref, inter_mem, local_sem.at[3]),
        pltpu.make_async_copy(
            template_ref.at[0, :, source_columns(me)],
            tbuf.at[me, :, window_columns(me)],
            local_sem.at[4],
        ),
        pltpu.make_async_copy(
            science_ref.at[0, 0, :, own_columns(me)], sbuf.at[me], local_sem.at[5]
        ),
    ]
    plan_in, orders_in, weight_in, inter_in, mine, mine_science = local
    for copy in local:
        copy.start()

    def template_copy(d, target, holder):
        return pltpu.make_async_remote_copy(
            src_ref=template_ref.at[0, :, source_columns(target)],
            dst_ref=tbuf.at[holder, :, window_columns(target)],
            send_sem=tsend.at[d],
            recv_sem=trecv.at[d],
            device_id={"expo": target},
            device_id_type=MESH,
        )

    def science_copy(d, target, holder):
        return pltpu.make_async_remote_copy(
            src_ref=science_ref.at[0, 0, :, own_columns(target)],
            dst_ref=sbuf.at[holder],
            send_sem=ssend.at[d],
            recv_sem=srecv.at[d],
            device_id={"expo": target},
            device_id_type=MESH,
        )

    def weight_copy(d, target, holder):
        return pltpu.make_async_remote_copy(
            src_ref=wbuf.at[holder],
            dst_ref=wbuf.at[holder],
            send_sem=wsend.at[d],
            recv_sem=wrecv.at[d],
            device_id={"expo": target},
            device_id_type=MESH,
        )

    def forward_copy(side):
        target = tile + 1 if side == 0 else tile - 1
        return pltpu.make_async_remote_copy(
            src_ref=picked.at[1],
            dst_ref=picked.at[2 * side],
            send_sem=fsend.at[side],
            recv_sem=frecv.at[side],
            device_id={"tile": target},
            device_id_type=MESH,
        )

    def stat_copy(index, e, t, to_e, to_t):
        return pltpu.make_async_remote_copy(
            src_ref=rbuf.at[e, t],
            dst_ref=rbuf.at[e, t],
            send_sem=rsend.at[index],
            recv_sem=rrecv.at[index],
            device_id={"expo": to_e, "tile": to_t},
            device_id_type=MESH,
        )

    pl.semaphore_wait(barrier, expos + 1)
    for d in reversed(range(1, expos)):

        @pl.when(me + d < expos)
        def _():
            template_copy(d, me + d, me).start()

        @pl.when(me - d >= 0)
        def _():
            template_copy(expos - d, me - d, me).start()

    for d in range(1, expos):
        science_copy(d, (me + d) % expos, me).start()
    weight_in.wait()
    inter_in.wait()
    weight = weight_mem[0, 0] * inter_mem[0, 0].astype(jnp.float32)
    wbuf[me] = jnp.full((1, LANES), weight, jnp.float32)
    for d in range(1, expos):
        weight_copy(d, (me + d) % expos, me).start()

    orders_in.wait()
    position = lax.broadcasted_iota(jnp.int32, (1, LANES), 1).astype(jnp.float32) - HALF
    for k in range(NB):
        sigma = SIGMAS[k]
        for side in range(2):
            order = orders_mem[side, k]
            line = taps(position, sigma, jnp.full((1, LANES), order, jnp.int32))
            scale = 1.0 / jnp.sqrt(jnp.sum(line * line, axis=1, keepdims=True))
            shape = (rows, 3 * rows) if side == 0 else (LANES + 2 * HALO, LANES)
            ahead = lax.broadcasted_iota(jnp.int32, shape, 1 - side)
            behind = lax.broadcasted_iota(jnp.int32, shape, side)
            offset = (ahead - behind - (rows if side == 0 else HALO)).astype(jnp.float32)
            band = taps(offset, sigma, jnp.full(shape, order, jnp.int32))
            band = (band * scale).astype(jnp.bfloat16)
            if side == 0:
                row_band[k * rows : (k + 1) * rows, :] = band
            else:
                col_band[k] = band

    @pl.when(tile == 0)
    def _():
        picked[0] = jnp.zeros((rows, keep), jnp.bfloat16)

    @pl.when(tile == tiles - 1)
    def _():
        picked[2] = jnp.zeros((rows, keep), jnp.bfloat16)

    plan_in.wait()
    owner = plan_mem[0]
    mine.wait()
    for d in range(1, expos):
        template_copy(d, me, (me + expos - d) % expos).wait_recv()

    block = tbuf[owner, :, LANES : LANES + span].astype(jnp.float32)
    place = jnp.full((rows, LANES), me, jnp.int32)
    block = jnp.concatenate(
        [
            jnp.where(place > 0, block[:, :LANES], 0.0),
            block[:, LANES : span - LANES],
            jnp.where(place < expos - 1, block[:, span - LANES :], 0.0),
        ],
        axis=1,
    )
    picked[1] = block[:, LANES - HALO : LANES - HALO + keep].astype(jnp.bfloat16)

    @pl.when(tile < tiles - 1)
    def _():
        forward_copy(0).start()

    @pl.when(tile > 0)
    def _():
        forward_copy(1).start()

    @pl.when(tile > 0)
    def _():
        forward_copy(0).wait_recv()

    @pl.when(tile < tiles - 1)
    def _():
        forward_copy(1).wait_recv()

    rowconv = jnp.dot(
        row_band[...], picked[...].reshape(3 * rows, keep), preferred_element_type=jnp.float32
    ).astype(jnp.bfloat16)
    for k in range(NB):
        mine_rows = rowconv[k * rows : (k + 1) * rows]
        windows = jnp.concatenate(
            [mine_rows[:, b * LANES : (b + 1) * LANES + 2 * HALO] for b in range(per)], axis=0
        )
        conv_ref[k] = jnp.dot(windows, col_band[k], preferred_element_type=jnp.float32)

    def conv_at(k, b):
        return conv_ref[k, b * rows : (b + 1) * rows, :]

    def science_at(e, b):
        return sbuf[e, :, b * LANES : (b + 1) * LANES].astype(jnp.float32)

    def fold(x):
        return x.reshape(rows // 8, 8, LANES).sum(axis=0)

    lane = lax.broadcasted_iota(jnp.int32, (1, LANES), 1)
    first = 2.0 * ((me * cols + lane).astype(jnp.float32) + 0.5) / width - 1.0
    pitch = 2.0 * LANES / width
    column = [first + b * pitch for b in range(per)]

    def running(tiles_of, depth):
        sums = [None] * depth
        for b in reversed(range(per)):
            carry = tiles_of(b)
            for level in range(depth):
                if level and b == 0:
                    break
                sums[level] = carry if sums[level] is None else sums[level] + carry
                carry = sums[level]
        return sums

    def once(sums):
        return first * sums[0] + pitch * sums[1]

    count = 3 * len(PAIRS) + 2 * NB
    first_twice = first * first
    first_once = 2.0 * pitch * first - pitch * pitch
    for index, (u, v) in enumerate(PAIRS):
        sums = running(lambda b: fold(conv_at(u, b) * conv_at(v, b)), 3)
        fold_ref[3 * index] = sums[0]
        fold_ref[3 * index + 1] = once(sums)
        fold_ref[3 * index + 2] = (
            first_twice * sums[0] + first_once * sums[1] + (2.0 * pitch * pitch) * sums[2]
        )
    for u in range(NB):
        sums = running(lambda b: fold(conv_at(u, b)), 2)
        fold_ref[3 * len(PAIRS) + u] = sums[0]
        fold_ref[3 * len(PAIRS) + NB + u] = once(sums)

    mine_science.wait()
    for d in range(1, expos):
        science_copy(d, me, (me + expos - d) % expos).wait_recv()
    for e in range(expos):
        science = [science_at(e, b) for b in range(per)]
        for u in range(NB):
            sums = running(lambda b: fold(conv_at(u, b) * science[b]), 2)
            fold_ref[count + u * expos + e] = sums[0]
            fold_ref[count + (NB + u) * expos + e] = once(sums)
        fold_ref[count + 2 * NB * expos + e] = running(lambda b: fold(science[b]), 1)[0]
    used = count + NU * expos
    for index in range(used, LANES):
        fold_ref[index] = jnp.zeros((8, LANES), jnp.float32)

    packed = jnp.concatenate(
        [sublane_sums([fold_ref[g + s] for s in range(8)]) for g in range(0, LANES, 8)], axis=0
    )
    rbuf[me, tile] = jnp.sum(jnp.transpose(packed), axis=0, keepdims=True)
    for index, e, t in others():
        stat_copy(index, me, tile, e, t).start()

    for d in range(1, expos):
        weight_copy(d, me, (me + expos - d) % expos).wait_recv()
    weights = [wbuf[e] for e in range(expos)]
    for b in range(per):
        result = science_at(0, b) * weights[0]
        for e in range(1, expos):
            result = result + science_at(e, b) * weights[e]
        coadd_ref[0, :, b * LANES : (b + 1) * LANES] = result

    for index, e, t in others():
        de, dt = index // tiles, index % tiles
        e = (me + expos - de) % expos
        t = (tile + tiles - dt) % tiles
        stat_copy(index, e, t, e, t).wait_recv()

    total = rbuf[0, 0]
    for e in range(expos):
        for t in range(tiles):
            if e or t:
                total = total + rbuf[e, t]
    stat_ref[...] = jnp.transpose(jnp.broadcast_to(total, (LANES, LANES)))

    def value(index):
        return jnp.broadcast_to(stat_ref[index : index + 1, :], (expos, LANES))

    matrix = [[None] * NU for _ in range(NU)]
    for index, (u, v) in enumerate(PAIRS):
        plain, linear, square = (value(3 * index + moment) for moment in range(3))
        matrix[u][v] = plain
        matrix[NB + u][v] = linear
        matrix[NB + v][u] = linear
        matrix[NB + u][NB + v] = square
    for u in range(2 * NB):
        matrix[2 * NB][u] = value(3 * len(PAIRS) + u)
    pixels = float(rows * tiles * width)
    matrix[2 * NB][2 * NB] = jnp.full((expos, LANES), pixels, jnp.float32)
    trace = matrix[0][0]
    for u in range(1, NU):
        trace = trace + matrix[u][u]
    ridge = RIDGE * (trace / NU)
    for u in range(NU):
        matrix[u][u] = matrix[u][u] + ridge
    right = [stat_ref[count + u * expos : count + (u + 1) * expos, :] for u in range(NU)]
    inverse = [None] * NU
    for j in range(NU):
        inverse[j] = 1.0 / matrix[j][j]
        for i in range(j + 1, NU):
            ratio = matrix[i][j] * inverse[j]
            for m in range(j + 1, i + 1):
                matrix[i][m] = matrix[i][m] - ratio * matrix[m][j]
            right[i] = right[i] - ratio * right[j]
    fitted = [None] * NU
    for j in reversed(range(NU)):
        left = right[j]
        for i in range(j + 1, NU):
            left = left - matrix[i][j] * fitted[i]
        fitted[j] = left * inverse[j]

    stacked = jnp.concatenate(weights, axis=0)
    joint = [jnp.sum(stacked * fitted[u], axis=0, keepdims=True) for u in range(NU)]
    for b in range(per):
        block = slice(b * LANES, (b + 1) * LANES)
        result = coadd_ref[0, :, block] - joint[2 * NB]
        for k in range(NB):
            factor = joint[k] + column[b] * joint[NB + k]
            result = result - conv_at(k, b) * factor
        coadd_ref[0, :, block] = result

    spread = lax.broadcasted_iota(jnp.int32, (expos, LANES), 1)
    table = jnp.zeros((expos, LANES), jnp.float32)
    for u in range(NU):
        table = jnp.where(spread == u, fitted[u], table)
    exposure = lax.broadcasted_iota(jnp.int32, (expos, LANES), 0)
    line = jnp.sum(jnp.where(exposure == me, table, 0.0), axis=0, keepdims=True)
    coeffs_ref[0] = line[:, :NU]

    for d in range(1, expos):
        template_copy(d, (me + d) % expos, me).wait_send()
        science_copy(d, (me + d) % expos, me).wait_send()
        weight_copy(d, (me + d) % expos, me).wait_send()

    @pl.when(tile < tiles - 1)
    def _():
        forward_copy(0).wait_send()

    @pl.when(tile > 0)
    def _():
        forward_copy(1).wait_send()

    for index, e, t in others():
        stat_copy(index, me, tile, e, t).wait_send()


def store(coadd_in, coeffs_in, coadd_out, coeffs_out, sem):
    copies = [
        pltpu.make_async_copy(coadd_in, coadd_out, sem.at[0]),
        pltpu.make_async_copy(coeffs_in, coeffs_out, sem.at[1]),
    ]
    for copy in copies:
        copy.start()
    for copy in copies:
        copy.wait()


def window(sizes, template, science, plan, orders, coadd_weight, intersection):
    expos, tiles = (sizes["expo"], sizes["tile"])
    rows, width = template.shape[1:]
    cols = width // expos
    fits = (
        science.shape[1] == 1
        and template.shape[0] == 1
        and expos > 2
        and tiles > 2
        and width % expos == 0
        and cols % LANES == 0
        and cols // LANES > 2
        and rows % 16 == 0
        and 3 * len(PAIRS) + 2 * NB + NU * expos <= LANES
    )
    if not fits:
        return per_device(template, science, plan, orders, coadd_weight, intersection)
    spare = 10368 * 1024
    dims = (expos, tiles, rows, width, cols)
    dma = pltpu.SemaphoreType.DMA
    far = pl.BlockSpec(memory_space=pltpu.HBM)
    vector = pl.BlockSpec(memory_space=pltpu.VMEM)
    shapes = (
        jax.ShapeDtypeStruct((1, rows, cols), jnp.float32),
        jax.ShapeDtypeStruct((1, 1, NU), jnp.float32),
    )
    plan, orders = (pltpu.with_memory_space_constraint(x, pltpu.HBM) for x in (plan, orders.T))
    results = pl.pallas_call(
        functools.partial(fused, dims),
        out_shape=shapes,
        in_specs=[far] * 6,
        out_specs=(vector, vector),
        scratch_shapes=[
            pltpu.VMEM((expos, rows, cols + 4 * LANES), jnp.bfloat16),
            pltpu.VMEM((3, rows, cols + 2 * HALO), jnp.bfloat16),
            pltpu.VMEM((expos, rows, cols), jnp.bfloat16),
            pltpu.VMEM((expos, 1, LANES), jnp.float32),
            pltpu.VMEM((expos, tiles, 1, LANES), jnp.float32),
            pltpu.VMEM((NB * rows, 3 * rows), jnp.bfloat16),
            pltpu.VMEM((NB, LANES + 2 * HALO, LANES), jnp.bfloat16),
            pltpu.VMEM((NB, rows * (cols // LANES), LANES), jnp.float32),
            pltpu.VMEM((LANES, 8, LANES), jnp.float32),
            pltpu.VMEM((LANES, LANES), jnp.float32),
            pltpu.SMEM(plan.shape, jnp.int32),
            pltpu.SMEM(orders.shape, jnp.int32),
            pltpu.SMEM(coadd_weight.shape, jnp.float32),
            pltpu.SMEM(intersection.shape, jnp.int32),
            dma((6,)),
            dma((expos,)),
            dma((expos,)),
            dma((expos,)),
            dma((expos,)),
            dma((expos,)),
            dma((expos,)),
            dma((2,)),
            dma((2,)),
            dma((expos * tiles,)),
            dma((expos * tiles,)),
        ],
        compiler_params=pltpu.CompilerParams(
            collective_id=0, has_side_effects=True, vmem_limit_bytes=VMEM_BYTES - spare
        ),
    )(template, science, plan, orders, coadd_weight, intersection)
    return pl.pallas_call(
        store,
        out_shape=shapes,
        in_specs=[vector, vector],
        out_specs=(far, far),
        scratch_shapes=[dma((2,))],
        compiler_params=pltpu.CompilerParams(vmem_limit_bytes=1024 * 1024),
    )(*results)


def solution(mesh):
    return jax.shard_map(
        functools.partial(window, dict(mesh.shape)),
        mesh=mesh,
        in_specs=(
            P(("groups", "expo"), "tile", None),
            P(("groups", "expo"), None, "tile", None),
            P("groups"),
            P(),
            P(("groups", "expo"), None),
            P(("groups", "expo"), None),
        ),
        out_specs=(P("groups", "tile", "expo"), P(("groups", "expo"), None, None)),
        check_vma=False,
    )
```

```python
import functools

import jax
import jax.numpy as jnp
from jax import lax
from jax.experimental import pallas as pl
from jax.experimental.pallas import tpu as pltpu
from jax.sharding import PartitionSpec as P

HALF = 15
NB = 6
NU = 13


SIGMAS = (0.8, 1.4, 2.2, 3.0, 4.0, 5.5)
RIDGE = 0.05


def broadcast(block, axis, holder):
    block = jnp.where(lax.axis_index(axis) == holder, block, jnp.zeros_like(block))
    return lax.psum(block, axis)


def extended(x, sides, width):
    for axis, dim in sides:
        size, length = (lax.axis_size(axis), x.shape[dim])
        up = [(i, (i + 1) % size) for i in range(size - 1)]
        down = [(j, i) for i, j in up]
        last = lax.slice_in_dim(x, length - width, length, axis=dim)
        first = lax.slice_in_dim(x, 0, width, axis=dim)
        before = lax.ppermute(last, axis, up)
        after = lax.ppermute(first, axis, down)
        x = jnp.concatenate([before, x, after], axis=dim)
    return x


def make_filters(orders):
    taps_pos = jnp.arange(2 * HALF + 1).astype(jnp.float32) - HALF
    row_list = []
    col_list = []
    for basis in range(NB):
        sigma = SIGMAS[basis]
        envelope = jnp.exp(-taps_pos * taps_pos / (2.0 * sigma * sigma))

        def power(order):
            return jnp.where(order == 0, 1.0, jnp.where(order == 1, taps_pos, taps_pos * taps_pos))

        row_filter = envelope * power(orders[basis, 0])
        col_filter = envelope * power(orders[basis, 1])
        row_list.append(row_filter / jnp.sqrt(jnp.sum(row_filter * row_filter)))
        col_list.append(col_filter / jnp.sqrt(jnp.sum(col_filter * col_filter)))
    return (jnp.stack(row_list).astype(jnp.bfloat16), jnp.stack(col_list).astype(jnp.bfloat16))


def band_matrix(filters, out_len, in_len):
    offset = jnp.arange(in_len)[None, :] - jnp.arange(out_len)[:, None]
    taps_idx = jnp.arange(2 * HALF + 1)
    picks = (offset[:, :, None] == taps_idx[None, None, :]).astype(jnp.float32)
    band = jnp.einsum("ijt,kt->kij", picks, filters.astype(jnp.float32))
    return band.astype(jnp.bfloat16)


def per_device(template, science, plan, orders, coadd_weight, intersection):
    row_filters, col_filters = make_filters(orders)
    rows = template.shape[1]
    width = template.shape[2]
    blocks_count = width // 128
    steps_count = science.shape[1]
    row_band = band_matrix(row_filters, rows, rows + 2 * HALF)
    col_band = jnp.transpose(band_matrix(col_filters, 128, 128 + 2 * HALF), (0, 2, 1))
    column_pos = 2.0 * (jnp.arange(width).astype(jnp.float32) + 0.5) / width - 1.0
    pieces = []
    fitted = []
    for step in range(steps_count):
        owner_index = plan[step]
        received = broadcast(template[0], "expo", owner_index)
        padded = extended(received, (("tile", 0),), HALF)
        rowconv = jnp.einsum(
            "kij,jw->kiw", row_band, padded, preferred_element_type=jnp.float32
        ).astype(jnp.bfloat16)
        blocks = rowconv.reshape(NB, rows, blocks_count, 128)
        empty_rim = jnp.zeros((NB, rows, 1, HALF), jnp.bfloat16)
        previous = jnp.concatenate([empty_rim, blocks[:, :, :-1, 128 - HALF :]], axis=2)
        following = jnp.concatenate([blocks[:, :, 1:, :HALF], empty_rim], axis=2)
        window = jnp.concatenate([previous, blocks, following], axis=3)
        conv = jnp.einsum("krbj,kjc->krbc", window, col_band, preferred_element_type=jnp.float32)
        conv = conv.reshape(NB, rows, width)
        fields = jnp.concatenate(
            [conv, conv * column_pos, jnp.ones((1, rows, width), jnp.float32)], axis=0
        )
        fields = fields.reshape(NU, rows * width)
        exposure_image = science[0, step].astype(jnp.float32).reshape(rows * width)
        normal_local = jnp.dot(fields, fields.T, precision=lax.Precision.HIGHEST)
        project_local = jnp.dot(fields, exposure_image, precision=lax.Precision.HIGHEST)
        normal_matrix, projections = lax.psum((normal_local, project_local), "tile")
        normal_matrix = normal_matrix + RIDGE * (jnp.trace(normal_matrix) / NU) * jnp.eye(
            NU, dtype=jnp.float32
        )
        factor = jnp.linalg.cholesky(normal_matrix)
        coeffs = jax.scipy.linalg.cho_solve((factor, True), projections)
        model = jnp.dot(coeffs, fields, precision=lax.Precision.HIGHEST)
        difference = exposure_image - model
        weight_now = coadd_weight[0, step] * intersection[0, step].astype(jnp.float32)
        pieces.append((weight_now * difference).reshape(rows, width))
        fitted.append(coeffs)
    weighted = jnp.stack(pieces)
    received_parts = lax.all_to_all(weighted[None], "expo", split_axis=3, concat_axis=0, tiled=True)
    coadd = jnp.sum(received_parts, axis=0)
    return (coadd, jnp.stack(fitted)[None])


LANES = 128
HALO = LANES // 2
VMEM_BYTES = 67043328
PAIRS = [(u, v) for u in range(NB) for v in range(u + 1)]
MESH = pl.DeviceIdType.MESH


def taps(position, sigma, order):
    power = jnp.where(order == 0, 1.0, jnp.where(order == 1, position, position * position))
    value = jnp.exp(-position * position / (2.0 * sigma * sigma)) * power
    return jnp.where(jnp.abs(position) <= HALF, value, 0.0)


def sublane_sums(tiles):
    row = lax.broadcasted_iota(jnp.int32, (8, LANES), 0)

    def merge(a, b, step):
        low = (row // step) % 2 == 0
        if step == 4:
            return jnp.where(low, a, b) + pltpu.roll(jnp.where(low, b, a), 4, 0)
        first = jnp.where(low, a, pltpu.roll(b, step, 0))
        return first + jnp.where(low, pltpu.roll(a, 8 - step, 0), b)

    fours = [merge(tiles[s], tiles[s + 4], 4) for s in range(4)]
    twos = [merge(fours[s], fours[s + 2], 2) for s in range(2)]
    return merge(twos[0], twos[1], 1)


def fused(
    dims,
    template_ref,
    science_ref,
    plan_ref,
    orders_ref,
    weight_ref,
    inter_ref,
    coadd_ref,
    coeffs_ref,
    template_mem,
    science_mem,
    shifted,
    tbuf,
    picked,
    sbuf,
    wbuf,
    rbuf,
    row_band,
    col_band,
    conv_ref,
    fold_ref,
    stat_ref,
    plan_mem,
    orders_mem,
    weight_mem,
    inter_mem,
    local_sem,
    tsend,
    trecv,
    ssend,
    srecv,
    wsend,
    wrecv,
    fsend,
    frecv,
    rsend,
    rrecv,
):
    expos, tiles, rows, width, cols = dims
    per = cols // LANES
    keep = cols + 2 * HALO
    me = lax.axis_index("expo")
    tile = lax.axis_index("tile")

    def others():
        near = [0] + list(range(2, expos - 1))
        for de in [expos - 1, 1][: expos - 1] + near[1:] + near[:1]:
            for dt in reversed(range(tiles)):
                if de or dt:
                    yield de * tiles + dt, (me + de) % expos, (tile + dt) % tiles

    barrier = pltpu.get_barrier_semaphore()

    for d in range(1, expos):
        peer = (me + d) % expos
        pl.semaphore_signal(barrier, inc=1, device_id={"expo": peer}, device_id_type=MESH)
    for d in (1, tiles - 1):
        peer = (tile + d) % tiles
        pl.semaphore_signal(barrier, inc=1, device_id={"tile": peer}, device_id_type=MESH)

    def shifted_columns(e):
        return pl.ds(pl.multiple_of(e * cols, LANES), keep)

    def own_columns(e):
        return pl.ds(pl.multiple_of(e * cols, LANES), cols)

    local = [
        pltpu.make_async_copy(plan_ref, plan_mem, local_sem.at[0]),
        pltpu.make_async_copy(orders_ref, orders_mem, local_sem.at[1]),
        pltpu.make_async_copy(weight_ref, weight_mem, local_sem.at[2]),
        pltpu.make_async_copy(inter_ref, inter_mem, local_sem.at[3]),
        pltpu.make_async_copy(
            science_ref.at[0, 0, :, own_columns(me)], sbuf.at[me], local_sem.at[4]
        ),
        pltpu.make_async_copy(template_ref.at[0], template_mem, local_sem.at[5]),
        pltpu.make_async_copy(science_ref.at[0, 0], science_mem, local_sem.at[6]),
    ]
    plan_in, orders_in, weight_in, inter_in, mine_science, template_in, science_in = local
    local = [template_in, science_in] + local[:5]
    mine = pltpu.make_async_copy(
        shifted.at[:, shifted_columns(me)], tbuf.at[me], local_sem.at[7]
    )
    for copy in local:
        copy.start()

    def template_copy(d, target, holder):
        return pltpu.make_async_remote_copy(
            src_ref=shifted.at[:, shifted_columns(target)],
            dst_ref=tbuf.at[holder],
            send_sem=tsend.at[d],
            recv_sem=trecv.at[d],
            device_id={"expo": target},
            device_id_type=MESH,
        )

    def science_copy(d, target, holder):
        return pltpu.make_async_remote_copy(
            src_ref=science_mem.at[:, own_columns(target)],
            dst_ref=sbuf.at[holder],
            send_sem=ssend.at[d],
            recv_sem=srecv.at[d],
            device_id={"expo": target},
            device_id_type=MESH,
        )

    def weight_copy(d, target, holder):
        return pltpu.make_async_remote_copy(
            src_ref=wbuf.at[holder],
            dst_ref=wbuf.at[holder],
            send_sem=wsend.at[d],
            recv_sem=wrecv.at[d],
            device_id={"expo": target},
            device_id_type=MESH,
        )

    def forward_copy(side):
        target = tile + 1 if side == 0 else tile - 1
        return pltpu.make_async_remote_copy(
            src_ref=picked.at[1],
            dst_ref=picked.at[2 * side],
            send_sem=fsend.at[side],
            recv_sem=frecv.at[side],
            device_id={"tile": target},
            device_id_type=MESH,
        )

    def stat_copy(index, e, t, to_e, to_t):
        return pltpu.make_async_remote_copy(
            src_ref=rbuf.at[e, t],
            dst_ref=rbuf.at[e, t],
            send_sem=rsend.at[index],
            recv_sem=rrecv.at[index],
            device_id={"expo": to_e, "tile": to_t},
            device_id_type=MESH,
        )

    template_in.wait()
    low = lax.broadcasted_iota(jnp.int32, (rows, LANES), 1) < HALO
    before = jnp.zeros((rows, LANES), jnp.float32)
    for start in range(0, width + LANES, LANES):
        after = jnp.zeros((rows, LANES), jnp.float32)
        if start < width:
            block = template_mem[:, start : start + LANES].astype(jnp.float32)
            after = pltpu.roll(block, HALO, 1)
        shifted[:, start : start + LANES] = jnp.where(low, before, after).astype(jnp.bfloat16)
        before = after

    pl.semaphore_wait(barrier, expos + 1)
    for d in reversed(range(1, expos)):

        @pl.when(me + d < expos)
        def _():
            template_copy(d, me + d, me).start()

        @pl.when(me - d >= 0)
        def _():
            template_copy(expos - d, me - d, me).start()

    mine.start()
    science_in.wait()
    for d in range(1, expos):
        science_copy(d, (me + d) % expos, me).start()
    weight_in.wait()
    inter_in.wait()
    weight = weight_mem[0, 0] * inter_mem[0, 0].astype(jnp.float32)
    wbuf[me] = jnp.full((1, LANES), weight, jnp.float32)
    for d in range(1, expos):
        weight_copy(d, (me + d) % expos, me).start()

    orders_in.wait()
    position = lax.broadcasted_iota(jnp.int32, (1, LANES), 1).astype(jnp.float32) - HALF
    for k in range(NB):
        sigma = SIGMAS[k]
        for side in range(2):
            order = orders_mem[side, k]
            line = taps(position, sigma, jnp.full((1, LANES), order, jnp.int32))
            scale = 1.0 / jnp.sqrt(jnp.sum(line * line, axis=1, keepdims=True))
            shape = (rows, 3 * rows) if side == 0 else (LANES + 2 * HALO, LANES)
            ahead = lax.broadcasted_iota(jnp.int32, shape, 1 - side)
            behind = lax.broadcasted_iota(jnp.int32, shape, side)
            offset = (ahead - behind - (rows if side == 0 else HALO)).astype(jnp.float32)
            band = taps(offset, sigma, jnp.full(shape, order, jnp.int32))
            band = (band * scale).astype(jnp.bfloat16)
            if side == 0:
                row_band[k * rows : (k + 1) * rows, :] = band
            else:
                col_band[k] = band

    @pl.when(tile == 0)
    def _():
        picked[0] = jnp.zeros((rows, keep), jnp.bfloat16)

    @pl.when(tile == tiles - 1)
    def _():
        picked[2] = jnp.zeros((rows, keep), jnp.bfloat16)

    plan_in.wait()
    owner = plan_mem[0]
    mine.wait()
    for d in range(1, expos):
        template_copy(d, me, (me + expos - d) % expos).wait_recv()

    picked[1] = tbuf[owner]

    @pl.when(tile < tiles - 1)
    def _():
        forward_copy(0).start()

    @pl.when(tile > 0)
    def _():
        forward_copy(1).start()

    @pl.when(tile > 0)
    def _():
        forward_copy(0).wait_recv()

    @pl.when(tile < tiles - 1)
    def _():
        forward_copy(1).wait_recv()

    rowconv = jnp.dot(
        row_band[...], picked[...].reshape(3 * rows, keep), preferred_element_type=jnp.float32
    ).astype(jnp.bfloat16)
    for k in range(NB):
        mine_rows = rowconv[k * rows : (k + 1) * rows]
        windows = jnp.concatenate(
            [mine_rows[:, b * LANES : (b + 1) * LANES + 2 * HALO] for b in range(per)], axis=0
        )
        conv_ref[k] = jnp.dot(windows, col_band[k], preferred_element_type=jnp.float32)

    def conv_at(k, b):
        return conv_ref[k, b * rows : (b + 1) * rows, :]

    def science_at(e, b):
        return sbuf[e, :, b * LANES : (b + 1) * LANES].astype(jnp.float32)

    def fold(x):
        return x.reshape(rows // 8, 8, LANES).sum(axis=0)

    lane = lax.broadcasted_iota(jnp.int32, (1, LANES), 1)
    first = 2.0 * ((me * cols + lane).astype(jnp.float32) + 0.5) / width - 1.0
    pitch = 2.0 * LANES / width
    column = [first + b * pitch for b in range(per)]

    def running(tiles_of, depth):
        sums = [None] * depth
        for b in reversed(range(per)):
            carry = tiles_of(b)
            for level in range(depth):
                if level and b == 0:
                    break
                sums[level] = carry if sums[level] is None else sums[level] + carry
                carry = sums[level]
        return sums

    def once(sums):
        return first * sums[0] + pitch * sums[1]

    count = 3 * len(PAIRS) + 2 * NB
    first_twice = first * first
    first_once = 2.0 * pitch * first - pitch * pitch
    for index, (u, v) in enumerate(PAIRS):
        sums = running(lambda b: fold(conv_at(u, b) * conv_at(v, b)), 3)
        fold_ref[3 * index] = sums[0]
        fold_ref[3 * index + 1] = once(sums)
        fold_ref[3 * index + 2] = (
            first_twice * sums[0] + first_once * sums[1] + (2.0 * pitch * pitch) * sums[2]
        )
    for u in range(NB):
        sums = running(lambda b: fold(conv_at(u, b)), 2)
        fold_ref[3 * len(PAIRS) + u] = sums[0]
        fold_ref[3 * len(PAIRS) + NB + u] = once(sums)

    mine_science.wait()
    for d in range(1, expos):
        science_copy(d, me, (me + expos - d) % expos).wait_recv()
    for e in range(expos):
        science = [science_at(e, b) for b in range(per)]
        for u in range(NB):
            sums = running(lambda b: fold(conv_at(u, b) * science[b]), 2)
            fold_ref[count + u * expos + e] = sums[0]
            fold_ref[count + (NB + u) * expos + e] = once(sums)
        fold_ref[count + 2 * NB * expos + e] = running(lambda b: fold(science[b]), 1)[0]
    used = count + NU * expos
    for index in range(used, LANES):
        fold_ref[index] = jnp.zeros((8, LANES), jnp.float32)

    packed = jnp.concatenate(
        [sublane_sums([fold_ref[g + s] for s in range(8)]) for g in range(0, LANES, 8)], axis=0
    )
    rbuf[me, tile] = jnp.sum(jnp.transpose(packed), axis=0, keepdims=True)
    for index, e, t in others():
        stat_copy(index, me, tile, e, t).start()

    for d in range(1, expos):
        weight_copy(d, me, (me + expos - d) % expos).wait_recv()
    weights = [wbuf[e] for e in range(expos)]
    for b in range(per):
        result = science_at(0, b) * weights[0]
        for e in range(1, expos):
            result = result + science_at(e, b) * weights[e]
        coadd_ref[0, :, b * LANES : (b + 1) * LANES] = result

    for index, e, t in others():
        de, dt = index // tiles, index % tiles
        e = (me + expos - de) % expos
        t = (tile + tiles - dt) % tiles
        stat_copy(index, e, t, e, t).wait_recv()

    total = rbuf[0, 0]
    for e in range(expos):
        for t in range(tiles):
            if e or t:
                total = total + rbuf[e, t]
    stat_ref[...] = jnp.transpose(jnp.broadcast_to(total, (LANES, LANES)))

    def value(index):
        return jnp.broadcast_to(stat_ref[index : index + 1, :], (expos, LANES))

    matrix = [[None] * NU for _ in range(NU)]
    for index, (u, v) in enumerate(PAIRS):
        plain, linear, square = (value(3 * index + moment) for moment in range(3))
        matrix[u][v] = plain
        matrix[NB + u][v] = linear
        matrix[NB + v][u] = linear
        matrix[NB + u][NB + v] = square
    for u in range(2 * NB):
        matrix[2 * NB][u] = value(3 * len(PAIRS) + u)
    pixels = float(rows * tiles * width)
    matrix[2 * NB][2 * NB] = jnp.full((expos, LANES), pixels, jnp.float32)
    trace = matrix[0][0]
    for u in range(1, NU):
        trace = trace + matrix[u][u]
    ridge = RIDGE * (trace / NU)
    for u in range(NU):
        matrix[u][u] = matrix[u][u] + ridge
    right = [stat_ref[count + u * expos : count + (u + 1) * expos, :] for u in range(NU)]
    inverse = [None] * NU
    for j in range(NU):
        inverse[j] = 1.0 / matrix[j][j]
        for i in range(j + 1, NU):
            ratio = matrix[i][j] * inverse[j]
            for m in range(j + 1, i + 1):
                matrix[i][m] = matrix[i][m] - ratio * matrix[m][j]
            right[i] = right[i] - ratio * right[j]
    fitted = [None] * NU
    for j in reversed(range(NU)):
        left = right[j]
        for i in range(j + 1, NU):
            left = left - matrix[i][j] * fitted[i]
        fitted[j] = left * inverse[j]

    stacked = jnp.concatenate(weights, axis=0)
    joint = [jnp.sum(stacked * fitted[u], axis=0, keepdims=True) for u in range(NU)]
    for b in range(per):
        block = slice(b * LANES, (b + 1) * LANES)
        result = coadd_ref[0, :, block] - joint[2 * NB]
        for k in range(NB):
            factor = joint[k] + column[b] * joint[NB + k]
            result = result - conv_at(k, b) * factor
        coadd_ref[0, :, block] = result

    spread = lax.broadcasted_iota(jnp.int32, (expos, LANES), 1)
    table = jnp.zeros((expos, LANES), jnp.float32)
    for u in range(NU):
        table = jnp.where(spread == u, fitted[u], table)
    exposure = lax.broadcasted_iota(jnp.int32, (expos, LANES), 0)
    line = jnp.sum(jnp.where(exposure == me, table, 0.0), axis=0, keepdims=True)
    coeffs_ref[0] = line[:, :NU]

    for d in range(1, expos):
        template_copy(d, (me + d) % expos, me).wait_send()
        science_copy(d, (me + d) % expos, me).wait_send()
        weight_copy(d, (me + d) % expos, me).wait_send()

    @pl.when(tile < tiles - 1)
    def _():
        forward_copy(0).wait_send()

    @pl.when(tile > 0)
    def _():
        forward_copy(1).wait_send()

    for index, e, t in others():
        stat_copy(index, me, tile, e, t).wait_send()


def store(coadd_in, coeffs_in, coadd_out, coeffs_out, sem):
    copies = [
        pltpu.make_async_copy(coadd_in, coadd_out, sem.at[0]),
        pltpu.make_async_copy(coeffs_in, coeffs_out, sem.at[1]),
    ]
    for copy in copies:
        copy.start()
    for copy in copies:
        copy.wait()


def window(sizes, template, science, plan, orders, coadd_weight, intersection):
    expos, tiles = (sizes["expo"], sizes["tile"])
    rows, width = template.shape[1:]
    cols = width // expos
    fits = (
        science.shape[1] == 1
        and template.shape[0] == 1
        and expos > 2
        and tiles > 2
        and width % expos == 0
        and cols % LANES == 0
        and cols // LANES > 2
        and rows % 16 == 0
        and 3 * len(PAIRS) + 2 * NB + NU * expos <= LANES
    )
    if not fits:
        return per_device(template, science, plan, orders, coadd_weight, intersection)
    spare = 10368 * 1024
    dims = (expos, tiles, rows, width, cols)
    dma = pltpu.SemaphoreType.DMA
    far = pl.BlockSpec(memory_space=pltpu.HBM)
    vector = pl.BlockSpec(memory_space=pltpu.VMEM)
    shapes = (
        jax.ShapeDtypeStruct((1, rows, cols), jnp.float32),
        jax.ShapeDtypeStruct((1, 1, NU), jnp.float32),
    )
    plan, orders = (pltpu.with_memory_space_constraint(x, pltpu.HBM) for x in (plan, orders.T))
    results = pl.pallas_call(
        functools.partial(fused, dims),
        out_shape=shapes,
        in_specs=[far] * 6,
        out_specs=(vector, vector),
        scratch_shapes=[
            pltpu.VMEM((rows, width), jnp.bfloat16),
            pltpu.VMEM((rows, width), jnp.bfloat16),
            pltpu.VMEM((rows, width + 2 * HALO), jnp.bfloat16),
            pltpu.VMEM((expos, rows, cols + 2 * HALO), jnp.bfloat16),
            pltpu.VMEM((3, rows, cols + 2 * HALO), jnp.bfloat16),
            pltpu.VMEM((expos, rows, cols), jnp.bfloat16),
            pltpu.VMEM((expos, 1, LANES), jnp.float32),
            pltpu.VMEM((expos, tiles, 1, LANES), jnp.float32),
            pltpu.VMEM((NB * rows, 3 * rows), jnp.bfloat16),
            pltpu.VMEM((NB, LANES + 2 * HALO, LANES), jnp.bfloat16),
            pltpu.VMEM((NB, rows * (cols // LANES), LANES), jnp.float32),
            pltpu.VMEM((LANES, 8, LANES), jnp.float32),
            pltpu.VMEM((LANES, LANES), jnp.float32),
            pltpu.SMEM(plan.shape, jnp.int32),
            pltpu.SMEM(orders.shape, jnp.int32),
            pltpu.SMEM(coadd_weight.shape, jnp.float32),
            pltpu.SMEM(intersection.shape, jnp.int32),
            dma((8,)),
            dma((expos,)),
            dma((expos,)),
            dma((expos,)),
            dma((expos,)),
            dma((expos,)),
            dma((expos,)),
            dma((2,)),
            dma((2,)),
            dma((expos * tiles,)),
            dma((expos * tiles,)),
        ],
        compiler_params=pltpu.CompilerParams(
            collective_id=0, has_side_effects=True, vmem_limit_bytes=VMEM_BYTES - spare
        ),
    )(template, science, plan, orders, coadd_weight, intersection)
    return pl.pallas_call(
        store,
        out_shape=shapes,
        in_specs=[vector, vector],
        out_specs=(far, far),
        scratch_shapes=[dma((2,))],
        compiler_params=pltpu.CompilerParams(vmem_limit_bytes=1024 * 1024),
    )(*results)


def solution(mesh):
    return jax.shard_map(
        functools.partial(window, dict(mesh.shape)),
        mesh=mesh,
        in_specs=(
            P(("groups", "expo"), "tile", None),
            P(("groups", "expo"), None, "tile", None),
            P("groups"),
            P(),
            P(("groups", "expo"), None),
            P(("groups", "expo"), None),
        ),
        out_specs=(P("groups", "tile", "expo"), P(("groups", "expo"), None, None)),
        check_vma=False,
    )
```

```python
import functools

import jax
import jax.numpy as jnp
from jax import lax
from jax.experimental import pallas as pl
from jax.experimental.pallas import tpu as pltpu
from jax.sharding import PartitionSpec as P

HALF = 15
NB = 6
NU = 13


SIGMAS = (0.8, 1.4, 2.2, 3.0, 4.0, 5.5)
RIDGE = 0.05


def broadcast(block, axis, holder):
    block = jnp.where(lax.axis_index(axis) == holder, block, jnp.zeros_like(block))
    return lax.psum(block, axis)


def extended(x, sides, width):
    for axis, dim in sides:
        size, length = (lax.axis_size(axis), x.shape[dim])
        up = [(i, (i + 1) % size) for i in range(size - 1)]
        down = [(j, i) for i, j in up]
        last = lax.slice_in_dim(x, length - width, length, axis=dim)
        first = lax.slice_in_dim(x, 0, width, axis=dim)
        before = lax.ppermute(last, axis, up)
        after = lax.ppermute(first, axis, down)
        x = jnp.concatenate([before, x, after], axis=dim)
    return x


def make_filters(orders):
    taps_pos = jnp.arange(2 * HALF + 1).astype(jnp.float32) - HALF
    row_list = []
    col_list = []
    for basis in range(NB):
        sigma = SIGMAS[basis]
        envelope = jnp.exp(-taps_pos * taps_pos / (2.0 * sigma * sigma))

        def power(order):
            return jnp.where(order == 0, 1.0, jnp.where(order == 1, taps_pos, taps_pos * taps_pos))

        row_filter = envelope * power(orders[basis, 0])
        col_filter = envelope * power(orders[basis, 1])
        row_list.append(row_filter / jnp.sqrt(jnp.sum(row_filter * row_filter)))
        col_list.append(col_filter / jnp.sqrt(jnp.sum(col_filter * col_filter)))
    return (jnp.stack(row_list).astype(jnp.bfloat16), jnp.stack(col_list).astype(jnp.bfloat16))


def band_matrix(filters, out_len, in_len):
    offset = jnp.arange(in_len)[None, :] - jnp.arange(out_len)[:, None]
    taps_idx = jnp.arange(2 * HALF + 1)
    picks = (offset[:, :, None] == taps_idx[None, None, :]).astype(jnp.float32)
    band = jnp.einsum("ijt,kt->kij", picks, filters.astype(jnp.float32))
    return band.astype(jnp.bfloat16)


def per_device(template, science, plan, orders, coadd_weight, intersection):
    row_filters, col_filters = make_filters(orders)
    rows = template.shape[1]
    width = template.shape[2]
    blocks_count = width // 128
    steps_count = science.shape[1]
    row_band = band_matrix(row_filters, rows, rows + 2 * HALF)
    col_band = jnp.transpose(band_matrix(col_filters, 128, 128 + 2 * HALF), (0, 2, 1))
    column_pos = 2.0 * (jnp.arange(width).astype(jnp.float32) + 0.5) / width - 1.0
    pieces = []
    fitted = []
    for step in range(steps_count):
        owner_index = plan[step]
        received = broadcast(template[0], "expo", owner_index)
        padded = extended(received, (("tile", 0),), HALF)
        rowconv = jnp.einsum(
            "kij,jw->kiw", row_band, padded, preferred_element_type=jnp.float32
        ).astype(jnp.bfloat16)
        blocks = rowconv.reshape(NB, rows, blocks_count, 128)
        empty_rim = jnp.zeros((NB, rows, 1, HALF), jnp.bfloat16)
        previous = jnp.concatenate([empty_rim, blocks[:, :, :-1, 128 - HALF :]], axis=2)
        following = jnp.concatenate([blocks[:, :, 1:, :HALF], empty_rim], axis=2)
        window = jnp.concatenate([previous, blocks, following], axis=3)
        conv = jnp.einsum("krbj,kjc->krbc", window, col_band, preferred_element_type=jnp.float32)
        conv = conv.reshape(NB, rows, width)
        fields = jnp.concatenate(
            [conv, conv * column_pos, jnp.ones((1, rows, width), jnp.float32)], axis=0
        )
        fields = fields.reshape(NU, rows * width)
        exposure_image = science[0, step].astype(jnp.float32).reshape(rows * width)
        normal_local = jnp.dot(fields, fields.T, precision=lax.Precision.HIGHEST)
        project_local = jnp.dot(fields, exposure_image, precision=lax.Precision.HIGHEST)
        normal_matrix, projections = lax.psum((normal_local, project_local), "tile")
        normal_matrix = normal_matrix + RIDGE * (jnp.trace(normal_matrix) / NU) * jnp.eye(
            NU, dtype=jnp.float32
        )
        factor = jnp.linalg.cholesky(normal_matrix)
        coeffs = jax.scipy.linalg.cho_solve((factor, True), projections)
        model = jnp.dot(coeffs, fields, precision=lax.Precision.HIGHEST)
        difference = exposure_image - model
        weight_now = coadd_weight[0, step] * intersection[0, step].astype(jnp.float32)
        pieces.append((weight_now * difference).reshape(rows, width))
        fitted.append(coeffs)
    weighted = jnp.stack(pieces)
    received_parts = lax.all_to_all(weighted[None], "expo", split_axis=3, concat_axis=0, tiled=True)
    coadd = jnp.sum(received_parts, axis=0)
    return (coadd, jnp.stack(fitted)[None])


LANES = 128
HALO = LANES // 2
VMEM_BYTES = 67043328
PAIRS = [(u, v) for u in range(NB) for v in range(u + 1)]
MESH = pl.DeviceIdType.MESH


def taps(position, sigma, order):
    power = jnp.where(order == 0, 1.0, jnp.where(order == 1, position, position * position))
    value = jnp.exp(-position * position / (2.0 * sigma * sigma)) * power
    return jnp.where(jnp.abs(position) <= HALF, value, 0.0)


def sublane_sums(tiles):
    row = lax.broadcasted_iota(jnp.int32, (8, LANES), 0)

    def merge(a, b, step):
        low = (row // step) % 2 == 0
        if step == 4:
            return jnp.where(low, a, b) + pltpu.roll(jnp.where(low, b, a), 4, 0)
        first = jnp.where(low, a, pltpu.roll(b, step, 0))
        return first + jnp.where(low, pltpu.roll(a, 8 - step, 0), b)

    fours = [merge(tiles[s], tiles[s + 4], 4) for s in range(4)]
    twos = [merge(fours[s], fours[s + 2], 2) for s in range(2)]
    return merge(twos[0], twos[1], 1)


def fused(
    dims,
    template_ref,
    science_ref,
    plan_ref,
    orders_ref,
    weight_ref,
    inter_ref,
    coadd_ref,
    coeffs_ref,
    template_mem,
    science_mem,
    shifted,
    tbuf,
    picked,
    sbuf,
    wbuf,
    rbuf,
    row_band,
    col_band,
    conv_ref,
    fold_ref,
    stat_ref,
    plan_mem,
    orders_mem,
    weight_mem,
    inter_mem,
    local_sem,
    tsend,
    trecv,
    ssend,
    srecv,
    wsend,
    wrecv,
    fsend,
    frecv,
    rsend,
    rrecv,
):
    expos, tiles, rows, width, cols = dims
    per = cols // LANES
    keep = cols + 2 * HALO
    me = lax.axis_index("expo")
    tile = lax.axis_index("tile")
    odd = tile % 2
    away = (1 - odd) * ((tile + tiles - 1) // tiles)
    near = tile + away

    def others():
        near = [0] + list(range(2, expos - 1))
        for de in [expos - 1, 1][: expos - 1] + near[1:] + near[:1]:
            for dt in reversed(range(tiles)):
                if de or dt:
                    yield de * tiles + dt, (me + de) % expos, (tile + dt) % tiles

    barrier = pltpu.get_barrier_semaphore()

    for d in range(1, expos):
        peer = (me + d) % expos
        pl.semaphore_signal(barrier, inc=1, device_id={"expo": peer}, device_id_type=MESH)
    @pl.when((odd == 1) & (tile > 1))
    def _():
        for d in range(1, expos):
            pl.semaphore_signal(
                barrier,
                inc=1,
                device_id={"expo": (me + d) % expos, "tile": tile - 1},
                device_id_type=MESH,
            )

    @pl.when((odd == 1) & (tile < tiles - 1))
    def _():
        pl.semaphore_signal(barrier, inc=1, device_id={"tile": tile + 2}, device_id_type=MESH)

    for d in (1, tiles - 1):
        peer = (tile + d) % tiles
        pl.semaphore_signal(barrier, inc=1, device_id={"tile": peer}, device_id_type=MESH)

    def shifted_columns(e):
        return pl.ds(pl.multiple_of(e * cols, LANES), keep)

    def own_columns(e):
        return pl.ds(pl.multiple_of(e * cols, LANES), cols)

    local = [
        pltpu.make_async_copy(plan_ref, plan_mem, local_sem.at[0]),
        pltpu.make_async_copy(orders_ref, orders_mem, local_sem.at[1]),
        pltpu.make_async_copy(weight_ref, weight_mem, local_sem.at[2]),
        pltpu.make_async_copy(inter_ref, inter_mem, local_sem.at[3]),
        pltpu.make_async_copy(
            science_ref.at[0, 0, :, own_columns(me)], sbuf.at[me], local_sem.at[4]
        ),
        pltpu.make_async_copy(template_ref.at[0], template_mem, local_sem.at[5]),
        pltpu.make_async_copy(science_ref.at[0, 0], science_mem, local_sem.at[6]),
    ]
    plan_in, orders_in, weight_in, inter_in, mine_science, template_in, science_in = local
    local = [template_in, science_in] + local[:5]
    mine = pltpu.make_async_copy(
        shifted.at[:, shifted_columns(me)], tbuf.at[me, 1], local_sem.at[7]
    )
    for copy in local:
        copy.start()

    def template_copy(d, target, holder):
        return pltpu.make_async_remote_copy(
            src_ref=shifted.at[:, shifted_columns(target)],
            dst_ref=tbuf.at[holder, 1 - away],
            send_sem=tsend.at[d],
            recv_sem=trecv.at[1 - away, d],
            device_id={"expo": target, "tile": near},
            device_id_type=MESH,
        )

    def template_arrival(side, d):
        landing = tbuf.at[(me + expos - d) % expos, side]
        return pltpu.make_async_remote_copy(
            src_ref=landing,
            dst_ref=landing,
            send_sem=tsend.at[d],
            recv_sem=trecv.at[side, d],
            device_id={"tile": tile - 1},
            device_id_type=MESH,
        )

    def science_copy(d, target, holder):
        return pltpu.make_async_remote_copy(
            src_ref=science_mem.at[:, own_columns(target)],
            dst_ref=sbuf.at[holder],
            send_sem=ssend.at[d],
            recv_sem=srecv.at[d],
            device_id={"expo": target},
            device_id_type=MESH,
        )

    def weight_copy(d, target, holder):
        return pltpu.make_async_remote_copy(
            src_ref=wbuf.at[holder],
            dst_ref=wbuf.at[holder],
            send_sem=wsend.at[d],
            recv_sem=wrecv.at[d],
            device_id={"expo": target},
            device_id_type=MESH,
        )

    def forward_copy(kind):
        ahead, source, landing = [(-2, 0, 2), (1, 1, 0), (-1, 0, 1), (-1, 1, 2)][kind]
        return pltpu.make_async_remote_copy(
            src_ref=picked.at[source],
            dst_ref=picked.at[landing],
            send_sem=fsend.at[kind],
            recv_sem=frecv.at[kind],
            device_id={"tile": tile + ahead},
            device_id_type=MESH,
        )

    def stat_copy(index, e, t, to_e, to_t):
        return pltpu.make_async_remote_copy(
            src_ref=rbuf.at[e, t],
            dst_ref=rbuf.at[e, t],
            send_sem=rsend.at[index],
            recv_sem=rrecv.at[index],
            device_id={"expo": to_e, "tile": to_t},
            device_id_type=MESH,
        )

    template_in.wait()
    low = lax.broadcasted_iota(jnp.int32, (rows, LANES), 1) < HALO
    before = jnp.zeros((rows, LANES), jnp.float32)
    for start in range(0, width + LANES, LANES):
        after = jnp.zeros((rows, LANES), jnp.float32)
        if start < width:
            block = template_mem[:, start : start + LANES].astype(jnp.float32)
            after = pltpu.roll(block, HALO, 1)
        shifted[:, start : start + LANES] = jnp.where(low, before, after).astype(jnp.bfloat16)
        before = after

    @pl.when(away == 1)
    def _():
        pl.semaphore_wait(barrier, 2 * expos)

    @pl.when(tile < 2)
    def _():
        pl.semaphore_wait(barrier, expos + 1)

    @pl.when((odd == 1) & (tile > 1))
    def _():
        pl.semaphore_wait(barrier, expos + 2)

    for d in reversed(range(1, expos)):
        template_copy(d, (me + d) % expos, me).start()

    @pl.when(away == 1)
    def _():
        template_copy(0, me, me).start()

    @pl.when(away == 0)
    def _():
        mine.start()

    science_in.wait()
    for d in range(1, expos):
        science_copy(d, (me + d) % expos, me).start()
    weight_in.wait()
    inter_in.wait()
    weight = weight_mem[0, 0] * inter_mem[0, 0].astype(jnp.float32)
    wbuf[me] = jnp.full((1, LANES), weight, jnp.float32)
    for d in range(1, expos):
        weight_copy(d, (me + d) % expos, me).start()

    orders_in.wait()
    position = lax.broadcasted_iota(jnp.int32, (1, LANES), 1).astype(jnp.float32) - HALF
    for k in range(NB):
        sigma = SIGMAS[k]
        for side in range(2):
            order = orders_mem[side, k]
            line = taps(position, sigma, jnp.full((1, LANES), order, jnp.int32))
            scale = 1.0 / jnp.sqrt(jnp.sum(line * line, axis=1, keepdims=True))
            shape = (rows, 3 * rows) if side == 0 else (LANES + 2 * HALO, LANES)
            ahead = lax.broadcasted_iota(jnp.int32, shape, 1 - side)
            behind = lax.broadcasted_iota(jnp.int32, shape, side)
            offset = (ahead - behind - (rows if side == 0 else HALO)).astype(jnp.float32)
            band = taps(offset, sigma, jnp.full(shape, order, jnp.int32))
            band = (band * scale).astype(jnp.bfloat16)
            if side == 0:
                row_band[k * rows : (k + 1) * rows, :] = band
            else:
                col_band[k] = band

    @pl.when(tile == 0)
    def _():
        picked[0] = jnp.zeros((rows, keep), jnp.bfloat16)

    @pl.when(tile == tiles - 1)
    def _():
        picked[2] = jnp.zeros((rows, keep), jnp.bfloat16)

    plan_in.wait()
    owner = plan_mem[0]

    @pl.when(away == 0)
    def _():
        mine.wait()
        for d in range(1, expos):
            template_arrival(1, d).wait_recv()

    @pl.when((odd == 1) & (tile > 1))
    def _():
        for d in range(expos):
            template_arrival(0, d).wait_recv()
        picked[0] = tbuf[owner, 0]
        forward_copy(0).start()
        forward_copy(2).start()

    @pl.when(away == 0)
    def _():
        picked[1] = tbuf[owner, 1]

        @pl.when(tile < tiles - 1)
        def _():
            forward_copy(1).start()

        @pl.when(tile > 0)
        def _():
            forward_copy(3).start()

    @pl.when((odd == 1) & (tile < tiles - 1))
    def _():
        forward_copy(0).wait_recv()

    @pl.when(away == 1)
    def _():
        forward_copy(2).wait_recv()

    @pl.when(odd == 0)
    def _():
        forward_copy(3).wait_recv()

    @pl.when((away == 1) | (tile == 1))
    def _():
        forward_copy(1).wait_recv()

    rowconv = jnp.dot(
        row_band[...], picked[...].reshape(3 * rows, keep), preferred_element_type=jnp.float32
    ).astype(jnp.bfloat16)
    for k in range(NB):
        mine_rows = rowconv[k * rows : (k + 1) * rows]
        windows = jnp.concatenate(
            [mine_rows[:, b * LANES : (b + 1) * LANES + 2 * HALO] for b in range(per)], axis=0
        )
        conv_ref[k] = jnp.dot(windows, col_band[k], preferred_element_type=jnp.float32)

    def conv_at(k, b):
        return conv_ref[k, b * rows : (b + 1) * rows, :]

    def science_at(e, b):
        return sbuf[e, :, b * LANES : (b + 1) * LANES].astype(jnp.float32)

    def fold(x):
        return x.reshape(rows // 8, 8, LANES).sum(axis=0)

    lane = lax.broadcasted_iota(jnp.int32, (1, LANES), 1)
    first = 2.0 * ((me * cols + lane).astype(jnp.float32) + 0.5) / width - 1.0
    pitch = 2.0 * LANES / width
    column = [first + b * pitch for b in range(per)]

    def running(tiles_of, depth):
        sums = [None] * depth
        for b in reversed(range(per)):
            carry = tiles_of(b)
            for level in range(depth):
                if level and b == 0:
                    break
                sums[level] = carry if sums[level] is None else sums[level] + carry
                carry = sums[level]
        return sums

    def once(sums):
        return first * sums[0] + pitch * sums[1]

    count = 3 * len(PAIRS) + 2 * NB
    first_twice = first * first
    first_once = 2.0 * pitch * first - pitch * pitch
    for index, (u, v) in enumerate(PAIRS):
        sums = running(lambda b: fold(conv_at(u, b) * conv_at(v, b)), 3)
        fold_ref[3 * index] = sums[0]
        fold_ref[3 * index + 1] = once(sums)
        fold_ref[3 * index + 2] = (
            first_twice * sums[0] + first_once * sums[1] + (2.0 * pitch * pitch) * sums[2]
        )
    for u in range(NB):
        sums = running(lambda b: fold(conv_at(u, b)), 2)
        fold_ref[3 * len(PAIRS) + u] = sums[0]
        fold_ref[3 * len(PAIRS) + NB + u] = once(sums)

    used = count + NU * expos
    for index in range(used, LANES):
        fold_ref[index] = jnp.zeros((8, LANES), jnp.float32)

    for d in range(expos):
        e = (me + expos - d) % expos
        if d == 0:
            mine_science.wait()
        else:
            science_copy(d, me, e).wait_recv()
        science = [science_at(e, b) for b in range(per)]
        for u in range(NB):
            sums = running(lambda b: fold(conv_at(u, b) * science[b]), 2)
            fold_ref[count + u * expos + e] = sums[0]
            fold_ref[count + (NB + u) * expos + e] = once(sums)
        fold_ref[count + 2 * NB * expos + e] = running(lambda b: fold(science[b]), 1)[0]

    packed = jnp.concatenate(
        [sublane_sums([fold_ref[g + s] for s in range(8)]) for g in range(0, LANES, 8)], axis=0
    )
    rbuf[me, tile] = jnp.sum(jnp.transpose(packed), axis=0, keepdims=True)
    for index, e, t in others():
        stat_copy(index, me, tile, e, t).start()

    for d in range(1, expos):
        weight_copy(d, me, (me + expos - d) % expos).wait_recv()
    weights = [wbuf[e] for e in range(expos)]
    for b in range(per):
        result = science_at(0, b) * weights[0]
        for e in range(1, expos):
            result = result + science_at(e, b) * weights[e]
        coadd_ref[0, :, b * LANES : (b + 1) * LANES] = result

    for index, e, t in others():
        de, dt = index // tiles, index % tiles
        e = (me + expos - de) % expos
        t = (tile + tiles - dt) % tiles
        stat_copy(index, e, t, e, t).wait_recv()

    total = rbuf[0, 0]
    for e in range(expos):
        for t in range(tiles):
            if e or t:
                total = total + rbuf[e, t]
    stat_ref[...] = jnp.transpose(jnp.broadcast_to(total, (LANES, LANES)))

    def value(index):
        return jnp.broadcast_to(stat_ref[index : index + 1, :], (expos, LANES))

    matrix = [[None] * NU for _ in range(NU)]
    for index, (u, v) in enumerate(PAIRS):
        plain, linear, square = (value(3 * index + moment) for moment in range(3))
        matrix[u][v] = plain
        matrix[NB + u][v] = linear
        matrix[NB + v][u] = linear
        matrix[NB + u][NB + v] = square
    for u in range(2 * NB):
        matrix[2 * NB][u] = value(3 * len(PAIRS) + u)
    pixels = float(rows * tiles * width)
    matrix[2 * NB][2 * NB] = jnp.full((expos, LANES), pixels, jnp.float32)
    trace = matrix[0][0]
    for u in range(1, NU):
        trace = trace + matrix[u][u]
    ridge = RIDGE * (trace / NU)
    for u in range(NU):
        matrix[u][u] = matrix[u][u] + ridge
    right = [stat_ref[count + u * expos : count + (u + 1) * expos, :] for u in range(NU)]
    inverse = [None] * NU
    for j in range(NU):
        inverse[j] = 1.0 / matrix[j][j]
        for i in range(j + 1, NU):
            ratio = matrix[i][j] * inverse[j]
            for m in range(j + 1, i + 1):
                matrix[i][m] = matrix[i][m] - ratio * matrix[m][j]
            right[i] = right[i] - ratio * right[j]
    fitted = [None] * NU
    for j in reversed(range(NU)):
        left = right[j]
        for i in range(j + 1, NU):
            left = left - matrix[i][j] * fitted[i]
        fitted[j] = left * inverse[j]

    stacked = jnp.concatenate(weights, axis=0)
    joint = [jnp.sum(stacked * fitted[u], axis=0, keepdims=True) for u in range(NU)]
    for b in range(per):
        block = slice(b * LANES, (b + 1) * LANES)
        result = coadd_ref[0, :, block] - joint[2 * NB]
        for k in range(NB):
            factor = joint[k] + column[b] * joint[NB + k]
            result = result - conv_at(k, b) * factor
        coadd_ref[0, :, block] = result

    spread = lax.broadcasted_iota(jnp.int32, (expos, LANES), 1)
    table = jnp.zeros((expos, LANES), jnp.float32)
    for u in range(NU):
        table = jnp.where(spread == u, fitted[u], table)
    exposure = lax.broadcasted_iota(jnp.int32, (expos, LANES), 0)
    line = jnp.sum(jnp.where(exposure == me, table, 0.0), axis=0, keepdims=True)
    coeffs_ref[0] = line[:, :NU]

    for d in range(1, expos):
        template_copy(d, (me + d) % expos, me).wait_send()
        science_copy(d, (me + d) % expos, me).wait_send()
        weight_copy(d, (me + d) % expos, me).wait_send()

    @pl.when(away == 1)
    def _():
        template_copy(0, me, me).wait_send()

    @pl.when((odd == 1) & (tile > 1))
    def _():
        forward_copy(0).wait_send()
        forward_copy(2).wait_send()

    @pl.when(away == 0)
    def _():
        @pl.when(tile < tiles - 1)
        def _():
            forward_copy(1).wait_send()

        @pl.when(tile > 0)
        def _():
            forward_copy(3).wait_send()

    for index, e, t in others():
        stat_copy(index, me, tile, e, t).wait_send()


def store(coadd_in, coeffs_in, coadd_out, coeffs_out, sem):
    copies = [
        pltpu.make_async_copy(coadd_in, coadd_out, sem.at[0]),
        pltpu.make_async_copy(coeffs_in, coeffs_out, sem.at[1]),
    ]
    for copy in copies:
        copy.start()
    for copy in copies:
        copy.wait()


def window(sizes, template, science, plan, orders, coadd_weight, intersection):
    expos, tiles = (sizes["expo"], sizes["tile"])
    rows, width = template.shape[1:]
    cols = width // expos
    fits = (
        science.shape[1] == 1
        and template.shape[0] == 1
        and expos > 2
        and tiles > 2
        and tiles == 4
        and width % expos == 0
        and cols % LANES == 0
        and cols // LANES > 2
        and rows % 16 == 0
        and 3 * len(PAIRS) + 2 * NB + NU * expos <= LANES
    )
    if not fits:
        return per_device(template, science, plan, orders, coadd_weight, intersection)
    spare = 10368 * 1024
    dims = (expos, tiles, rows, width, cols)
    dma = pltpu.SemaphoreType.DMA
    far = pl.BlockSpec(memory_space=pltpu.HBM)
    vector = pl.BlockSpec(memory_space=pltpu.VMEM)
    shapes = (
        jax.ShapeDtypeStruct((1, rows, cols), jnp.float32),
        jax.ShapeDtypeStruct((1, 1, NU), jnp.float32),
    )
    plan, orders = (pltpu.with_memory_space_constraint(x, pltpu.HBM) for x in (plan, orders.T))
    results = pl.pallas_call(
        functools.partial(fused, dims),
        out_shape=shapes,
        in_specs=[far] * 6,
        out_specs=(vector, vector),
        scratch_shapes=[
            pltpu.VMEM((rows, width), jnp.bfloat16),
            pltpu.VMEM((rows, width), jnp.bfloat16),
            pltpu.VMEM((rows, width + 2 * HALO), jnp.bfloat16),
            pltpu.VMEM((expos, 2, rows, cols + 2 * HALO), jnp.bfloat16),
            pltpu.VMEM((3, rows, cols + 2 * HALO), jnp.bfloat16),
            pltpu.VMEM((expos, rows, cols), jnp.bfloat16),
            pltpu.VMEM((expos, 1, LANES), jnp.float32),
            pltpu.VMEM((expos, tiles, 1, LANES), jnp.float32),
            pltpu.VMEM((NB * rows, 3 * rows), jnp.bfloat16),
            pltpu.VMEM((NB, LANES + 2 * HALO, LANES), jnp.bfloat16),
            pltpu.VMEM((NB, rows * (cols // LANES), LANES), jnp.float32),
            pltpu.VMEM((LANES, 8, LANES), jnp.float32),
            pltpu.VMEM((LANES, LANES), jnp.float32),
            pltpu.SMEM(plan.shape, jnp.int32),
            pltpu.SMEM(orders.shape, jnp.int32),
            pltpu.SMEM(coadd_weight.shape, jnp.float32),
            pltpu.SMEM(intersection.shape, jnp.int32),
            dma((8,)),
            dma((expos,)),
            dma((2, expos)),
            dma((expos,)),
            dma((expos,)),
            dma((expos,)),
            dma((expos,)),
            dma((4,)),
            dma((4,)),
            dma((expos * tiles,)),
            dma((expos * tiles,)),
        ],
        compiler_params=pltpu.CompilerParams(
            collective_id=0, has_side_effects=True, vmem_limit_bytes=VMEM_BYTES - spare
        ),
    )(template, science, plan, orders, coadd_weight, intersection)
    return pl.pallas_call(
        store,
        out_shape=shapes,
        in_specs=[vector, vector],
        out_specs=(far, far),
        scratch_shapes=[dma((2,))],
        compiler_params=pltpu.CompilerParams(vmem_limit_bytes=1024 * 1024),
    )(*results)


def solution(mesh):
    return jax.shard_map(
        functools.partial(window, dict(mesh.shape)),
        mesh=mesh,
        in_specs=(
            P(("groups", "expo"), "tile", None),
            P(("groups", "expo"), None, "tile", None),
            P("groups"),
            P(),
            P(("groups", "expo"), None),
            P(("groups", "expo"), None),
        ),
        out_specs=(P("groups", "tile", "expo"), P(("groups", "expo"), None, None)),
        check_vma=False,
    )
```

```python
import functools

import jax
import jax.numpy as jnp
from jax import lax
from jax.experimental import pallas as pl
from jax.experimental.pallas import tpu as pltpu
from jax.sharding import PartitionSpec as P

HALF = 15
NB = 6
NU = 13


SIGMAS = (0.8, 1.4, 2.2, 3.0, 4.0, 5.5)
RIDGE = 0.05


def broadcast(block, axis, holder):
    block = jnp.where(lax.axis_index(axis) == holder, block, jnp.zeros_like(block))
    return lax.psum(block, axis)


def extended(x, sides, width):
    for axis, dim in sides:
        size, length = (lax.axis_size(axis), x.shape[dim])
        up = [(i, (i + 1) % size) for i in range(size - 1)]
        down = [(j, i) for i, j in up]
        last = lax.slice_in_dim(x, length - width, length, axis=dim)
        first = lax.slice_in_dim(x, 0, width, axis=dim)
        before = lax.ppermute(last, axis, up)
        after = lax.ppermute(first, axis, down)
        x = jnp.concatenate([before, x, after], axis=dim)
    return x


def make_filters(orders):
    taps_pos = jnp.arange(2 * HALF + 1).astype(jnp.float32) - HALF
    row_list = []
    col_list = []
    for basis in range(NB):
        sigma = SIGMAS[basis]
        envelope = jnp.exp(-taps_pos * taps_pos / (2.0 * sigma * sigma))

        def power(order):
            return jnp.where(order == 0, 1.0, jnp.where(order == 1, taps_pos, taps_pos * taps_pos))

        row_filter = envelope * power(orders[basis, 0])
        col_filter = envelope * power(orders[basis, 1])
        row_list.append(row_filter / jnp.sqrt(jnp.sum(row_filter * row_filter)))
        col_list.append(col_filter / jnp.sqrt(jnp.sum(col_filter * col_filter)))
    return (jnp.stack(row_list).astype(jnp.bfloat16), jnp.stack(col_list).astype(jnp.bfloat16))


def band_matrix(filters, out_len, in_len):
    offset = jnp.arange(in_len)[None, :] - jnp.arange(out_len)[:, None]
    taps_idx = jnp.arange(2 * HALF + 1)
    picks = (offset[:, :, None] == taps_idx[None, None, :]).astype(jnp.float32)
    band = jnp.einsum("ijt,kt->kij", picks, filters.astype(jnp.float32))
    return band.astype(jnp.bfloat16)


def per_device(template, science, plan, orders, coadd_weight, intersection):
    row_filters, col_filters = make_filters(orders)
    rows = template.shape[1]
    width = template.shape[2]
    blocks_count = width // 128
    steps_count = science.shape[1]
    row_band = band_matrix(row_filters, rows, rows + 2 * HALF)
    col_band = jnp.transpose(band_matrix(col_filters, 128, 128 + 2 * HALF), (0, 2, 1))
    column_pos = 2.0 * (jnp.arange(width).astype(jnp.float32) + 0.5) / width - 1.0
    pieces = []
    fitted = []
    for step in range(steps_count):
        owner_index = plan[step]
        received = broadcast(template[0], "expo", owner_index)
        padded = extended(received, (("tile", 0),), HALF)
        rowconv = jnp.einsum(
            "kij,jw->kiw", row_band, padded, preferred_element_type=jnp.float32
        ).astype(jnp.bfloat16)
        blocks = rowconv.reshape(NB, rows, blocks_count, 128)
        empty_rim = jnp.zeros((NB, rows, 1, HALF), jnp.bfloat16)
        previous = jnp.concatenate([empty_rim, blocks[:, :, :-1, 128 - HALF :]], axis=2)
        following = jnp.concatenate([blocks[:, :, 1:, :HALF], empty_rim], axis=2)
        window = jnp.concatenate([previous, blocks, following], axis=3)
        conv = jnp.einsum("krbj,kjc->krbc", window, col_band, preferred_element_type=jnp.float32)
        conv = conv.reshape(NB, rows, width)
        fields = jnp.concatenate(
            [conv, conv * column_pos, jnp.ones((1, rows, width), jnp.float32)], axis=0
        )
        fields = fields.reshape(NU, rows * width)
        exposure_image = science[0, step].astype(jnp.float32).reshape(rows * width)
        normal_local = jnp.dot(fields, fields.T, precision=lax.Precision.HIGHEST)
        project_local = jnp.dot(fields, exposure_image, precision=lax.Precision.HIGHEST)
        normal_matrix, projections = lax.psum((normal_local, project_local), "tile")
        normal_matrix = normal_matrix + RIDGE * (jnp.trace(normal_matrix) / NU) * jnp.eye(
            NU, dtype=jnp.float32
        )
        factor = jnp.linalg.cholesky(normal_matrix)
        coeffs = jax.scipy.linalg.cho_solve((factor, True), projections)
        model = jnp.dot(coeffs, fields, precision=lax.Precision.HIGHEST)
        difference = exposure_image - model
        weight_now = coadd_weight[0, step] * intersection[0, step].astype(jnp.float32)
        pieces.append((weight_now * difference).reshape(rows, width))
        fitted.append(coeffs)
    weighted = jnp.stack(pieces)
    received_parts = lax.all_to_all(weighted[None], "expo", split_axis=3, concat_axis=0, tiled=True)
    coadd = jnp.sum(received_parts, axis=0)
    return (coadd, jnp.stack(fitted)[None])


LANES = 128
HALO = LANES // 2
VMEM_BYTES = 67043328
PAIRS = [(u, v) for u in range(NB) for v in range(u + 1)]
MESH = pl.DeviceIdType.MESH


def taps(position, sigma, order):
    power = jnp.where(order == 0, 1.0, jnp.where(order == 1, position, position * position))
    value = jnp.exp(-position * position / (2.0 * sigma * sigma)) * power
    return jnp.where(jnp.abs(position) <= HALF, value, 0.0)


def sublane_sums(tiles):
    row = lax.broadcasted_iota(jnp.int32, (8, LANES), 0)

    def merge(a, b, step):
        low = (row // step) % 2 == 0
        if step == 4:
            return jnp.where(low, a, b) + pltpu.roll(jnp.where(low, b, a), 4, 0)
        first = jnp.where(low, a, pltpu.roll(b, step, 0))
        return first + jnp.where(low, pltpu.roll(a, 8 - step, 0), b)

    fours = [merge(tiles[s], tiles[s + 4], 4) for s in range(4)]
    twos = [merge(fours[s], fours[s + 2], 2) for s in range(2)]
    return merge(twos[0], twos[1], 1)


def fused(
    dims,
    template_ref,
    science_ref,
    plan_ref,
    orders_ref,
    weight_ref,
    inter_ref,
    coadd_ref,
    coeffs_ref,
    template_mem,
    science_mem,
    shifted,
    tbuf,
    picked,
    sbuf,
    wbuf,
    rbuf,
    row_band,
    col_band,
    conv_ref,
    fold_ref,
    stat_ref,
    plan_mem,
    orders_mem,
    weight_mem,
    inter_mem,
    local_sem,
    tsend,
    trecv,
    ssend,
    srecv,
    wsend,
    wrecv,
    fsend,
    frecv,
    rsend,
    rrecv,
):
    expos, tiles, rows, width, cols = dims
    per = cols // LANES
    keep = cols + 2 * HALO
    me = lax.axis_index("expo")
    tile = lax.axis_index("tile")

    def others():
        near = [0] + list(range(2, expos - 1))
        for de in [expos - 1, 1][: expos - 1] + near[1:] + near[:1]:
            for dt in reversed(range(tiles)):
                if de or dt:
                    yield de * tiles + dt, (me + de) % expos, (tile + dt) % tiles

    barrier = pltpu.get_barrier_semaphore()

    for d in range(1, expos):
        peer = (me + d) % expos
        pl.semaphore_signal(barrier, inc=1, device_id={"expo": peer}, device_id_type=MESH)
    for d in (1, tiles - 1):
        peer = (tile + d) % tiles
        pl.semaphore_signal(barrier, inc=1, device_id={"tile": peer}, device_id_type=MESH)

    def shifted_columns(e):
        return pl.ds(pl.multiple_of(e * cols, LANES), keep)

    def own_columns(e):
        return pl.ds(pl.multiple_of(e * cols, LANES), cols)

    local = [
        pltpu.make_async_copy(plan_ref, plan_mem, local_sem.at[0]),
        pltpu.make_async_copy(orders_ref, orders_mem, local_sem.at[1]),
        pltpu.make_async_copy(weight_ref, weight_mem, local_sem.at[2]),
        pltpu.make_async_copy(inter_ref, inter_mem, local_sem.at[3]),
        pltpu.make_async_copy(
            science_ref.at[0, 0, :, own_columns(me)], sbuf.at[me], local_sem.at[4]
        ),
        pltpu.make_async_copy(template_ref.at[0], template_mem, local_sem.at[5]),
        pltpu.make_async_copy(science_ref.at[0, 0], science_mem, local_sem.at[6]),
    ]
    plan_in, orders_in, weight_in, inter_in, mine_science, template_in, science_in = local
    local = [template_in, science_in] + local[:5]
    mine = pltpu.make_async_copy(
        shifted.at[:, shifted_columns(me)], tbuf.at[me], local_sem.at[7]
    )
    for copy in local:
        copy.start()

    def template_copy(d, target, holder):
        return pltpu.make_async_remote_copy(
            src_ref=shifted.at[:, shifted_columns(target)],
            dst_ref=tbuf.at[holder],
            send_sem=tsend.at[d],
            recv_sem=trecv.at[d],
            device_id={"expo": target},
            device_id_type=MESH,
        )

    def science_copy(d, target, holder):
        return pltpu.make_async_remote_copy(
            src_ref=science_mem.at[:, own_columns(target)],
            dst_ref=sbuf.at[holder],
            send_sem=ssend.at[d],
            recv_sem=srecv.at[d],
            device_id={"expo": target},
            device_id_type=MESH,
        )

    def weight_copy(d, target, holder):
        return pltpu.make_async_remote_copy(
            src_ref=wbuf.at[holder],
            dst_ref=wbuf.at[holder],
            send_sem=wsend.at[d],
            recv_sem=wrecv.at[d],
            device_id={"expo": target},
            device_id_type=MESH,
        )

    def forward_copy(side):
        target = tile + 1 if side == 0 else tile - 1
        return pltpu.make_async_remote_copy(
            src_ref=picked.at[1],
            dst_ref=picked.at[2 * side],
            send_sem=fsend.at[side],
            recv_sem=frecv.at[side],
            device_id={"tile": target},
            device_id_type=MESH,
        )

    def stat_copy(index, e, t, to_e, to_t):
        return pltpu.make_async_remote_copy(
            src_ref=rbuf.at[e, t],
            dst_ref=rbuf.at[e, t],
            send_sem=rsend.at[index],
            recv_sem=rrecv.at[index],
            device_id={"expo": to_e, "tile": to_t},
            device_id_type=MESH,
        )

    template_in.wait()
    low = lax.broadcasted_iota(jnp.int32, (rows, LANES), 1) < HALO
    before = jnp.zeros((rows, LANES), jnp.float32)
    for start in range(0, width + LANES, LANES):
        after = jnp.zeros((rows, LANES), jnp.float32)
        if start < width:
            block = template_mem[:, start : start + LANES].astype(jnp.float32)
            after = pltpu.roll(block, HALO, 1)
        shifted[:, start : start + LANES] = jnp.where(low, before, after).astype(jnp.bfloat16)
        before = after

    pl.semaphore_wait(barrier, expos + 1)
    for d in reversed(range(1, expos)):

        @pl.when(me + d < expos)
        def _():
            template_copy(d, me + d, me).start()

        @pl.when(me - d >= 0)
        def _():
            template_copy(expos - d, me - d, me).start()

    mine.start()
    science_in.wait()
    for d in range(1, expos):
        science_copy(d, (me + d) % expos, me).start()
    weight_in.wait()
    inter_in.wait()
    weight = weight_mem[0, 0] * inter_mem[0, 0].astype(jnp.float32)
    wbuf[me] = jnp.full((1, LANES), weight, jnp.float32)
    for d in range(1, expos):
        weight_copy(d, (me + d) % expos, me).start()

    orders_in.wait()
    position = lax.broadcasted_iota(jnp.int32, (1, LANES), 1).astype(jnp.float32) - HALF
    for k in range(NB):
        sigma = SIGMAS[k]
        for side in range(2):
            order = orders_mem[side, k]
            line = taps(position, sigma, jnp.full((1, LANES), order, jnp.int32))
            scale = 1.0 / jnp.sqrt(jnp.sum(line * line, axis=1, keepdims=True))
            shape = (rows, 3 * rows) if side == 0 else (LANES + 2 * HALO, LANES)
            ahead = lax.broadcasted_iota(jnp.int32, shape, 1 - side)
            behind = lax.broadcasted_iota(jnp.int32, shape, side)
            offset = (ahead - behind - (rows if side == 0 else HALO)).astype(jnp.float32)
            band = taps(offset, sigma, jnp.full(shape, order, jnp.int32))
            band = (band * scale).astype(jnp.bfloat16)
            if side == 0:
                row_band[k * rows : (k + 1) * rows, :] = band
            else:
                col_band[k] = band

    @pl.when(tile == 0)
    def _():
        picked[0] = jnp.zeros((rows, keep), jnp.bfloat16)

    @pl.when(tile == tiles - 1)
    def _():
        picked[2] = jnp.zeros((rows, keep), jnp.bfloat16)

    plan_in.wait()
    owner = plan_mem[0]
    mine.wait()
    for d in range(1, expos):
        template_copy(d, me, (me + expos - d) % expos).wait_recv()

    picked[1] = tbuf[owner]

    @pl.when(tile < tiles - 1)
    def _():
        forward_copy(0).start()

    @pl.when(tile > 0)
    def _():
        forward_copy(1).start()

    @pl.when(tile > 0)
    def _():
        forward_copy(0).wait_recv()

    @pl.when(tile < tiles - 1)
    def _():
        forward_copy(1).wait_recv()

    rowconv = jnp.dot(
        row_band[...], picked[...].reshape(3 * rows, keep), preferred_element_type=jnp.float32
    ).astype(jnp.bfloat16)
    for k in range(NB):
        mine_rows = rowconv[k * rows : (k + 1) * rows]
        windows = jnp.concatenate(
            [mine_rows[:, b * LANES : (b + 1) * LANES + 2 * HALO] for b in range(per)], axis=0
        )
        conv_ref[k] = jnp.dot(windows, col_band[k], preferred_element_type=jnp.float32)

    def conv_at(k, b):
        return conv_ref[k, b * rows : (b + 1) * rows, :]

    def science_at(e, b):
        return sbuf[e, :, b * LANES : (b + 1) * LANES].astype(jnp.float32)

    def fold(x):
        return x.reshape(rows // 8, 8, LANES).sum(axis=0)

    lane = lax.broadcasted_iota(jnp.int32, (1, LANES), 1)
    first = 2.0 * ((me * cols + lane).astype(jnp.float32) + 0.5) / width - 1.0
    pitch = 2.0 * LANES / width
    column = [first + b * pitch for b in range(per)]

    def running(tiles_of, depth):
        sums = [None] * depth
        for b in reversed(range(per)):
            carry = tiles_of(b)
            for level in range(depth):
                if level and b == 0:
                    break
                sums[level] = carry if sums[level] is None else sums[level] + carry
                carry = sums[level]
        return sums

    def once(sums):
        return first * sums[0] + pitch * sums[1]

    count = 3 * len(PAIRS) + 2 * NB
    first_twice = first * first
    first_once = 2.0 * pitch * first - pitch * pitch
    for index, (u, v) in enumerate(PAIRS):
        sums = running(lambda b: fold(conv_at(u, b) * conv_at(v, b)), 3)
        fold_ref[3 * index] = sums[0]
        fold_ref[3 * index + 1] = once(sums)
        fold_ref[3 * index + 2] = (
            first_twice * sums[0] + first_once * sums[1] + (2.0 * pitch * pitch) * sums[2]
        )
    for u in range(NB):
        sums = running(lambda b: fold(conv_at(u, b)), 2)
        fold_ref[3 * len(PAIRS) + u] = sums[0]
        fold_ref[3 * len(PAIRS) + NB + u] = once(sums)

    used = count + NU * expos
    for index in range(used, LANES):
        fold_ref[index] = jnp.zeros((8, LANES), jnp.float32)

    for d in range(expos):
        e = (me + expos - d) % expos
        if d == 0:
            mine_science.wait()
        else:
            science_copy(d, me, e).wait_recv()
        science = [science_at(e, b) for b in range(per)]
        for u in range(NB):
            sums = running(lambda b: fold(conv_at(u, b) * science[b]), 2)
            fold_ref[count + u * expos + e] = sums[0]
            fold_ref[count + (NB + u) * expos + e] = once(sums)
        fold_ref[count + 2 * NB * expos + e] = running(lambda b: fold(science[b]), 1)[0]

    packed = jnp.concatenate(
        [sublane_sums([fold_ref[g + s] for s in range(8)]) for g in range(0, LANES, 8)], axis=0
    )
    rbuf[me, tile] = jnp.sum(jnp.transpose(packed), axis=0, keepdims=True)
    for index, e, t in others():
        stat_copy(index, me, tile, e, t).start()

    for d in range(1, expos):
        weight_copy(d, me, (me + expos - d) % expos).wait_recv()
    weights = [wbuf[e] for e in range(expos)]
    for b in range(per):
        result = science_at(0, b) * weights[0]
        for e in range(1, expos):
            result = result + science_at(e, b) * weights[e]
        coadd_ref[0, :, b * LANES : (b + 1) * LANES] = result

    for index, e, t in others():
        de, dt = index // tiles, index % tiles
        e = (me + expos - de) % expos
        t = (tile + tiles - dt) % tiles
        stat_copy(index, e, t, e, t).wait_recv()

    total = rbuf[0, 0]
    for e in range(expos):
        for t in range(tiles):
            if e or t:
                total = total + rbuf[e, t]
    stat_ref[...] = jnp.transpose(jnp.broadcast_to(total, (LANES, LANES)))

    def value(index):
        return jnp.broadcast_to(stat_ref[index : index + 1, :], (expos, LANES))

    matrix = [[None] * NU for _ in range(NU)]
    for index, (u, v) in enumerate(PAIRS):
        plain, linear, square = (value(3 * index + moment) for moment in range(3))
        matrix[u][v] = plain
        matrix[NB + u][v] = linear
        matrix[NB + v][u] = linear
        matrix[NB + u][NB + v] = square
    for u in range(2 * NB):
        matrix[2 * NB][u] = value(3 * len(PAIRS) + u)
    pixels = float(rows * tiles * width)
    matrix[2 * NB][2 * NB] = jnp.full((expos, LANES), pixels, jnp.float32)
    trace = matrix[0][0]
    for u in range(1, NU):
        trace = trace + matrix[u][u]
    ridge = RIDGE * (trace / NU)
    for u in range(NU):
        matrix[u][u] = matrix[u][u] + ridge
    right = [stat_ref[count + u * expos : count + (u + 1) * expos, :] for u in range(NU)]
    inverse = [None] * NU
    for j in range(NU):
        inverse[j] = 1.0 / matrix[j][j]
        for i in range(j + 1, NU):
            ratio = matrix[i][j] * inverse[j]
            for m in range(j + 1, i + 1):
                matrix[i][m] = matrix[i][m] - ratio * matrix[m][j]
            right[i] = right[i] - ratio * right[j]
    fitted = [None] * NU
    for j in reversed(range(NU)):
        left = right[j]
        for i in range(j + 1, NU):
            left = left - matrix[i][j] * fitted[i]
        fitted[j] = left * inverse[j]

    stacked = jnp.concatenate(weights, axis=0)
    joint = [jnp.sum(stacked * fitted[u], axis=0, keepdims=True) for u in range(NU)]
    for b in range(per):
        block = slice(b * LANES, (b + 1) * LANES)
        result = coadd_ref[0, :, block] - joint[2 * NB]
        for k in range(NB):
            factor = joint[k] + column[b] * joint[NB + k]
            result = result - conv_at(k, b) * factor
        coadd_ref[0, :, block] = result

    spread = lax.broadcasted_iota(jnp.int32, (expos, LANES), 1)
    table = jnp.zeros((expos, LANES), jnp.float32)
    for u in range(NU):
        table = jnp.where(spread == u, fitted[u], table)
    exposure = lax.broadcasted_iota(jnp.int32, (expos, LANES), 0)
    line = jnp.sum(jnp.where(exposure == me, table, 0.0), axis=0, keepdims=True)
    coeffs_ref[0] = line[:, :NU]

    for d in range(1, expos):
        template_copy(d, (me + d) % expos, me).wait_send()
        science_copy(d, (me + d) % expos, me).wait_send()
        weight_copy(d, (me + d) % expos, me).wait_send()

    @pl.when(tile < tiles - 1)
    def _():
        forward_copy(0).wait_send()

    @pl.when(tile > 0)
    def _():
        forward_copy(1).wait_send()

    for index, e, t in others():
        stat_copy(index, me, tile, e, t).wait_send()


def store(coadd_in, coeffs_in, coadd_out, coeffs_out, sem):
    copies = [
        pltpu.make_async_copy(coadd_in, coadd_out, sem.at[0]),
        pltpu.make_async_copy(coeffs_in, coeffs_out, sem.at[1]),
    ]
    for copy in copies:
        copy.start()
    for copy in copies:
        copy.wait()


def window(sizes, template, science, plan, orders, coadd_weight, intersection):
    expos, tiles = (sizes["expo"], sizes["tile"])
    rows, width = template.shape[1:]
    cols = width // expos
    fits = (
        science.shape[1] == 1
        and template.shape[0] == 1
        and expos > 2
        and tiles > 2
        and width % expos == 0
        and cols % LANES == 0
        and cols // LANES > 2
        and rows % 16 == 0
        and 3 * len(PAIRS) + 2 * NB + NU * expos <= LANES
    )
    if not fits:
        return per_device(template, science, plan, orders, coadd_weight, intersection)
    spare = 10368 * 1024
    dims = (expos, tiles, rows, width, cols)
    dma = pltpu.SemaphoreType.DMA
    far = pl.BlockSpec(memory_space=pltpu.HBM)
    vector = pl.BlockSpec(memory_space=pltpu.VMEM)
    shapes = (
        jax.ShapeDtypeStruct((1, rows, cols), jnp.float32),
        jax.ShapeDtypeStruct((1, 1, NU), jnp.float32),
    )
    plan, orders = (pltpu.with_memory_space_constraint(x, pltpu.HBM) for x in (plan, orders.T))
    results = pl.pallas_call(
        functools.partial(fused, dims),
        out_shape=shapes,
        in_specs=[far] * 6,
        out_specs=(vector, vector),
        scratch_shapes=[
            pltpu.VMEM((rows, width), jnp.bfloat16),
            pltpu.VMEM((rows, width), jnp.bfloat16),
            pltpu.VMEM((rows, width + 2 * HALO), jnp.bfloat16),
            pltpu.VMEM((expos, rows, cols + 2 * HALO), jnp.bfloat16),
            pltpu.VMEM((3, rows, cols + 2 * HALO), jnp.bfloat16),
            pltpu.VMEM((expos, rows, cols), jnp.bfloat16),
            pltpu.VMEM((expos, 1, LANES), jnp.float32),
            pltpu.VMEM((expos, tiles, 1, LANES), jnp.float32),
            pltpu.VMEM((NB * rows, 3 * rows), jnp.bfloat16),
            pltpu.VMEM((NB, LANES + 2 * HALO, LANES), jnp.bfloat16),
            pltpu.VMEM((NB, rows * (cols // LANES), LANES), jnp.float32),
            pltpu.VMEM((LANES, 8, LANES), jnp.float32),
            pltpu.VMEM((LANES, LANES), jnp.float32),
            pltpu.SMEM(plan.shape, jnp.int32),
            pltpu.SMEM(orders.shape, jnp.int32),
            pltpu.SMEM(coadd_weight.shape, jnp.float32),
            pltpu.SMEM(intersection.shape, jnp.int32),
            dma((8,)),
            dma((expos,)),
            dma((expos,)),
            dma((expos,)),
            dma((expos,)),
            dma((expos,)),
            dma((expos,)),
            dma((2,)),
            dma((2,)),
            dma((expos * tiles,)),
            dma((expos * tiles,)),
        ],
        compiler_params=pltpu.CompilerParams(
            collective_id=0, has_side_effects=True, vmem_limit_bytes=VMEM_BYTES - spare
        ),
    )(template, science, plan, orders, coadd_weight, intersection)
    return pl.pallas_call(
        store,
        out_shape=shapes,
        in_specs=[vector, vector],
        out_specs=(far, far),
        scratch_shapes=[dma((2,))],
        compiler_params=pltpu.CompilerParams(vmem_limit_bytes=1024 * 1024),
    )(*results)


def solution(mesh):
    return jax.shard_map(
        functools.partial(window, dict(mesh.shape)),
        mesh=mesh,
        in_specs=(
            P(("groups", "expo"), "tile", None),
            P(("groups", "expo"), None, "tile", None),
            P("groups"),
            P(),
            P(("groups", "expo"), None),
            P(("groups", "expo"), None),
        ),
        out_specs=(P("groups", "tile", "expo"), P(("groups", "expo"), None, None)),
        check_vma=False,
    )
```
